256 devices in a mesh: gx: 8 (over x_lo, y), gy: 32 (over x_hi, z, core).
Axes of the slice: x: 4 (x_hi: 2, x_lo: 2; x = x_hi * 2 + x_lo), y: 4, z: 8, core: 2. Of those that a mesh axis runs over, the one named last changes fastest.
Arguments:
- u_face: float32 [8, 2048, 2048], P(None, 'gy', 'gx'), may hold values from -6 to 6
- v_face: float32 [8, 2048, 2048], P(None, 'gy', 'gx'), may hold values from -6 to 6
- w_face: float32 [8, 2048, 2048], P(None, 'gy', 'gx'), may hold values from -6 to 6
- theta_field: float32 [8, 2048, 2048], P(None, 'gy', 'gx'), may hold values from -6 to 6
- density: float32 [8], replicated, may hold values from 0.3 to 1.5
- thickness: float32 [8], replicated, may hold values from 4 to 32
Outputs:
- u_new: float32 [8, 2048, 2048], P(None, 'gy', 'gx')
- v_new: float32 [8, 2048, 2048], P(None, 'gy', 'gx')
- w_new: float32 [8, 2048, 2048], P(None, 'gy', 'gx')
- theta_new: float32 [8, 2048, 2048], P(None, 'gy', 'gx')
- pressure: float32 [8, 2048, 2048], P(None, 'gy', 'gx')
The draws below stay inside these ranges and needn't reach their ends.
All inputs are finite; a program needn't handle non-finite values.
Results may differ from the reference program's by a relative error of at most 0.0003.
Values sent between devices are 32-bit elements; how exact they have to be, the bound alone decides.
A program may use at most 64 MiB of HBM per device.

```python
import math
import jax
import jax.numpy as jnp

NX = 2048
NY = 2048
NZ = 8


def draw_w_face(key, part):
    values = jnp.clip(jax.random.normal(key, (NZ, NY, NX), jnp.float32), -6.0, 6.0)
    return values


def block_levels(rng, extent, shards, least, top_value):
    loudness = 1.0
    for axis_at, blocks in shards:
        draws = jax.random.uniform(jax.random.fold_in(jax.random.fold_in(rng, 6), axis_at), (blocks,), jnp.float32, least / len(shards), top_value / len(shards))
        loudness = loudness * jnp.repeat(jnp.exp(draws), extent[axis_at] // blocks).reshape((-1,) + (1,) * (len(extent) - 1 - axis_at))
    return loudness


def scatter_about(key, dims, scale, most, pieces=(), kind=jnp.bfloat16):
    factor_of = block_levels(key, dims, pieces, -0.22, 0.18) if pieces else 1.0
    result = jax.random.normal(key, dims, jnp.float32) * scale * factor_of
    return jnp.minimum(jnp.maximum(result, -most), most).astype(kind)


def setup_inputs(seed: int = 0) -> dict:
    splits = jax.random.split(jax.random.key(seed), 7)
    u_face = scatter_about(splits[0], (NZ, NY, NX), 1.0, 6.0, ((1, 32), (2, 8)), jnp.float32)
    v_face = scatter_about(splits[1], (NZ, NY, NX), 1.0, 6.0, ((1, 32), (2, 8)), jnp.float32)
    w_face = draw_w_face(jax.random.fold_in(splits[6], 71), 0)
    theta_field = scatter_about(splits[3], (NZ, NY, NX), 1.0, 6.0, ((1, 32), (2, 8)), jnp.float32)
    density = jnp.clip(jnp.exp(jax.random.uniform(splits[4], (NZ,), jnp.float32, math.log(0.3), math.log(1.5))), 0.3, 1.5)
    thickness = jnp.clip(jnp.exp(jax.random.uniform(splits[5], (NZ,), jnp.float32, math.log(4.0), math.log(32.0))), 4.0, 32.0)
    return dict(u_face=u_face, v_face=v_face, w_face=w_face, theta_field=theta_field, density=density, thickness=thickness)


time_step = 0.2
buoyancy_gain = 1.0


def lift_level(field):
    return jnp.concatenate([field[1:], field[-1:]], axis=0)


def upwind_flux(q_m2, q_m1, q_zero, q_p1, q_p2, q_p3, velocity):
    centred = velocity * (37.0 * (q_zero + q_p1) - 8.0 * (q_m1 + q_p2) + (q_m2 + q_p3)) / 60.0
    damped = jnp.abs(velocity) * (10.0 * (q_p1 - q_zero) - 5.0 * (q_p2 - q_m1) + (q_p3 - q_m2)) / 60.0
    return centred - damped


def vertical_tend(tracer, velocity, rho_face, rho_level, spacing):
    levels = tracer.shape[0]
    padded = jnp.pad(tracer, ((2, 3), (0, 0), (0, 0)), mode="edge")
    parts = [padded[2 + offset:2 + offset + levels] for offset in range(-2, 4)]
    flux_z = upwind_flux(*parts, velocity) * rho_face[:, None, None]
    below = jnp.concatenate([jnp.zeros_like(flux_z[:1]), flux_z[:-1]], axis=0)
    return -(flux_z - below) / (rho_level * spacing)[:, None, None]


def horizontal_tend(tracer, u_vel, v_vel):
    parts_x = [jnp.roll(tracer, -offset, axis=2) for offset in range(-2, 4)]
    flux_x = upwind_flux(*parts_x, u_vel)
    parts_y = [jnp.roll(tracer, -offset, axis=1) for offset in range(-2, 4)]
    flux_y = upwind_flux(*parts_y, v_vel)
    return -(flux_x - jnp.roll(flux_x, 1, axis=2)) - (flux_y - jnp.roll(flux_y, 1, axis=1))


def hartley(field, axis):
    spectrum = jnp.fft.fft(field, axis=axis)
    return jnp.real(spectrum) - jnp.imag(spectrum)


def tridiag_solve(lower_coef, upper_coef, eigen_sum, source_term):
    levels = source_term.shape[0]
    shape_b = (levels,) + (1,) * (source_term.ndim - 1)
    low_b = lower_coef.reshape(shape_b)
    high_b = upper_coef.reshape(shape_b)
    ratios = []
    partial_sols = []
    for level in range(levels):
        pivots = eigen_sum - low_b[level] - high_b[level]
        numerator = source_term[level]
        if level > 0:
            pivots = pivots - low_b[level] * ratios[-1]
            numerator = numerator - low_b[level] * partial_sols[-1]
        ratios.append(high_b[level] / pivots)
        partial_sols.append(numerator / pivots)
    solved_levels = [partial_sols[-1]]
    for level in range(levels - 2, -1, -1):
        solved_levels.append(partial_sols[level] - ratios[level] * solved_levels[-1])
    return jnp.stack(solved_levels[::-1], axis=0)


def eigen_line(indices, count):
    return -4.0 * jnp.sin(math.pi * indices / count) ** 2


def reference(u_face, v_face, w_face, theta_field, density, thickness):
    face_density = (density + lift_level(density)) / 2.0
    face_spacing = (thickness + lift_level(thickness)) / 2.0
    adv_theta = horizontal_tend(theta_field, u_face, v_face) + vertical_tend(theta_field, w_face, face_density, density, thickness)
    u_level = (u_face + lift_level(u_face)) / 2.0
    v_level = (v_face + lift_level(v_face)) / 2.0
    w_level = (w_face + lift_level(w_face)) / 2.0
    adv_w = horizontal_tend(w_face, u_level, v_level) + vertical_tend(w_face, w_level, lift_level(density), face_density, face_spacing)
    theta_new = theta_field + time_step * adv_theta
    w_star = w_face + time_step * (adv_w + buoyancy_gain * (theta_field + lift_level(theta_field)) / 2.0)
    mass_flux = face_density[:, None, None] * w_star
    mass_below = jnp.concatenate([jnp.zeros_like(mass_flux[:1]), mass_flux[:-1]], axis=0)
    divergence = (u_face - jnp.roll(u_face, 1, axis=2)) + (v_face - jnp.roll(v_face, 1, axis=1))
    divergence = divergence + (mass_flux - mass_below) / (density * thickness)[:, None, None]
    source_term = divergence / time_step
    spectra = hartley(hartley(source_term, 2), 1)
    eig_x = eigen_line(jnp.arange(NX, dtype=jnp.int32), NX)
    eig_y = eigen_line(jnp.arange(NY, dtype=jnp.int32), NY)
    eigen_sum = eig_y[:, None] + eig_x[None, :]
    lower_coef = jnp.concatenate([jnp.zeros((1,), density.dtype), face_density[:-1] / (density[1:] * thickness[1:] * face_spacing[:-1])])
    upper_coef = face_density / (density * thickness * face_spacing)
    solution = tridiag_solve(lower_coef, upper_coef, eigen_sum, spectra)
    pressure = hartley(hartley(solution, 1), 2) / (NX * NY)
    u_new = u_face - time_step * (jnp.roll(pressure, -1, axis=2) - pressure)
    v_new = v_face - time_step * (jnp.roll(pressure, -1, axis=1) - pressure)
    above = jnp.concatenate([pressure[1:], jnp.zeros_like(pressure[:1])], axis=0)
    w_new = w_star - time_step * (above - pressure) / face_spacing[:, None, None]
    return (u_new, v_new, w_new, theta_new, pressure)
```

```python
import functools

import jax
import jax.numpy as jnp
import numpy as np
from jax import lax
from jax.experimental import pallas as pl
from jax.experimental.pallas import tpu as pltpu
from jax.sharding import PartitionSpec as P

DT = 0.2
f32 = jnp.float32
bf16 = jnp.bfloat16
MESH = pl.DeviceIdType.MESH
C1, C2, C3 = float(np.cos(np.pi / 8)), float(np.cos(np.pi / 4)), float(np.cos(3 * np.pi / 8))
YC = 16


def split_bf16(a):
    hi = a.astype(jnp.bfloat16)
    lo = (a - hi.astype(np.float64)).astype(jnp.bfloat16)
    return hi, lo


@functools.cache
def tables():
    n_x = 2048
    l = np.arange(128)
    n = np.arange(128)

    def cas(t):
        return np.cos(t) + np.sin(t)

    cos = np.cos(2 * np.pi * np.outer(l, n) / 128)
    sin = np.sin(2 * np.pi * np.outer(l, n) / 128)
    zero = np.zeros((128, 128))
    fw = np.block([[cos, -sin], [sin, cos]])
    b0 = cas(2 * np.pi * np.outer(l, n) / 128)
    b8 = cas(2 * np.pi * np.outer(l, 16 * n + 8) / n_x)
    fb = np.block([[b0, zero], [zero, b8]])
    mats = []
    for m in (fw, fb, fw.T * (2 / n_x), fb.T * (1 / n_x)):
        mats.extend(split_bf16(m))
    mats = np.stack(mats)
    tw = np.arange(8)[:, None] * l[None, :] * (2 * np.pi / n_x)
    k_lo = 16 * n[None, :] + np.arange(8)[:, None]
    k_hi = k_lo.copy()
    k_hi[0] += 8
    tab = np.concatenate(
        [np.cos(tw), np.sin(tw), 4 * np.sin(np.pi * k_lo / n_x) ** 2, 4 * np.sin(np.pi * k_hi / n_x) ** 2]
    ).astype(np.float32)
    return mats, tab


def fwd16(x):
    s = [x[q] + x[q + 8] for q in range(8)]
    d = [x[q] - x[q + 8] for q in range(8)]
    t = [s[q] + s[q + 4] for q in range(4)]
    e = [s[q] - s[q + 4] for q in range(4)]
    t02, t13 = t[0] + t[2], t[1] + t[3]
    re, im = {}, {}
    y0, y8 = t02 + t13, t02 - t13
    re[4], im[4] = t[0] - t[2], t[3] - t[1]
    a, b = C2 * (e[1] - e[3]), C2 * (e[1] + e[3])
    re[2], re[6] = e[0] + a, e[0] - a
    im[2], im[6] = -(e[2] + b), e[2] - b
    u = [None] + [d[q] - d[8 - q] for q in (1, 2, 3)]
    v = [None] + [d[q] + d[8 - q] for q in (1, 2, 3)]
    g = C2 * u[2]
    g1, g2 = d[0] + g, d[0] - g
    h1, h2 = C1 * u[1] + C3 * u[3], C3 * u[1] - C1 * u[3]
    re[1], re[7], re[3], re[5] = g1 + h1, g1 - h1, g2 + h2, g2 - h2
    k = C2 * v[2]
    k1, k2 = k + d[4], k - d[4]
    m1, m2 = C3 * v[1] + C1 * v[3], C1 * v[1] - C3 * v[3]
    im[1], im[7], im[3], im[5] = -(m1 + k1), k1 - m1, -(m2 + k2), k2 - m2
    return y0, y8, re, im


def inv16(a0, a8, zr, zi):
    p1, m1, p3, m3 = zr[1] + zr[7], zr[1] - zr[7], zr[3] + zr[5], zr[3] - zr[5]
    r1, s1, r3, s3 = zi[1] + zi[7], zi[1] - zi[7], zi[3] + zi[5], zi[3] - zi[5]
    o = [None] * 8
    o[0] = p1 + p3
    o[4] = s3 - s1
    cs = [None, C1 * m1 + C3 * m3, C2 * (p1 - p3), C3 * m1 - C1 * m3]
    sn = [None, C3 * r1 + C1 * r3, C2 * (s1 + s3), C1 * r1 - C3 * r3]
    for q in (1, 2, 3):
        o[q] = cs[q] - sn[q]
        o[8 - q] = -cs[q] - sn[q]
    ap, am = a0 + a8, a0 - a8
    g = [ap + zr[4], am - zi[4], ap - zr[4], am + zi[4]]
    w1, w2 = C2 * (zr[2] - zr[6]), C2 * (zi[2] + zi[6])
    h = [zr[2] + zr[6], w1 - w2, zi[6] - zi[2], -w1 - w2]
    ev = [g[q] + h[q] for q in range(4)] + [g[q] - h[q] for q in range(4)]
    return [ev[q] + o[q] for q in range(8)] + [ev[q] - o[q] for q in range(8)]


def dot3(x, hi, lo):
    xh = x.astype(bf16)
    xl = (x - xh.astype(f32)).astype(bf16)
    out = jnp.dot(xh, hi, preferred_element_type=f32)
    out += jnp.dot(xl, hi, preferred_element_type=f32)
    out += jnp.dot(xh, lo, preferred_element_type=f32)
    return out


def flux(qm2, qm1, q0, q1, q2, q3, c):
    s = 37.0 * (q0 + q1) - 8.0 * (qm1 + q2) + (qm2 + q3)
    d = 10.0 * (q1 - q0) - 5.0 * (q2 - qm1) + (q3 - qm2)
    return c * s - jnp.abs(c) * d


def roll(x, shift, axis):
    n = x.shape[axis]
    shift = shift % n
    return x if shift == 0 else pltpu.roll(x, shift, axis)


def lanes(shape):
    return lax.broadcasted_iota(jnp.int32, shape, len(shape) - 1)


def rows_of(shape):
    return lax.broadcasted_iota(jnp.int32, shape, 0)


def kernel(
    nx_dev, ny_dev,
    den_ref, thk_ref, tab_ref, u_hbm, v_hbm, w_hbm, th_hbm, mats_hbm,
    un_ref, vn_ref, wn_ref, tn_ref, p_ref,
    U, V, W, TH, MATS, COEF, TF, TI, LAM,
    PE_S, PW_S, PE_R, PW_R, YN_S, YS_S, YN_R, YS_R, FPK, FYP,
    WS, SRC, TX1, RX1, Z, S, SB, IFS, IFR, IFO, IFB, RP, TX2, RX2, X2, XR, EW, EC, EX,
    in_sem, hs_sem, hr_sem, s1_sem, r1_sem, l1_sem, is_sem, ir_sem, s2_sem, r2_sem, l2_sem,
    sx_sem, rx_sem,
):
    gx = lax.axis_index("gx")
    gy = lax.axis_index("gy")
    levels, ny, nx = u_hbm.shape
    chunks = ny // YC

    def px(t):
        return lax.rem(gx + t, nx_dev)

    def py(t):
        return lax.rem(gy + t, ny_dev)

    mid = pl.ds(8, ny)
    loads = [
        pltpu.make_async_copy(w_hbm, W.at[:, mid, :], in_sem.at[0]),
        pltpu.make_async_copy(th_hbm, TH.at[:, mid, :], in_sem.at[1]),
        pltpu.make_async_copy(u_hbm, U, in_sem.at[2]),
        pltpu.make_async_copy(v_hbm, V.at[:, mid, :], in_sem.at[3]),
        pltpu.make_async_copy(mats_hbm, MATS, in_sem.at[4]),
    ]
    for cp in loads:
        cp.start()

    barrier = pltpu.get_barrier_semaphore()
    for t in range(1, nx_dev):
        pl.semaphore_signal(barrier, inc=1, device_id={"gx": px(t)}, device_id_type=MESH)

    @pl.loop(1, ny_dev)
    def _(t):
        pl.semaphore_signal(barrier, inc=1, device_id={"gy": py(t)}, device_id_type=MESH)

    r8 = rows_of((8, 128))
    j8 = lax.rem(lanes((8, 128)), 8)
    den = jnp.zeros((8, 128), f32)
    thk = jnp.zeros((8, 128), f32)
    for k in range(levels):
        den = jnp.where(r8 == k, den_ref[k], den)
        thk = jnp.where(r8 == k, thk_ref[k], thk)

    def lift(a):
        return jnp.where(r8 == 7, a, roll(a, -1, 0))

    def below(a):
        return jnp.where(r8 == 0, 0.0, roll(a, 1, 0))

    lden = lift(den)
    fd = (den + lden) / 2.0
    fs = (thk + lift(thk)) / 2.0
    mass = den * thk
    zw = (DT / 60.0) / (fd * fs)
    zt = (DT / 60.0) / mass
    sc = (1.0 / DT) / mass
    coefs = [lden * zw, below(lden) * zw, fd * zt, below(fd) * zt, fd * sc, below(fd) * sc, DT / fs]
    for i, a in enumerate(coefs):
        COEF[i * 8 : i * 8 + 8, :] = jnp.concatenate([a, a], axis=1)

    cond = fd / fs
    diag = jnp.sqrt(cond / mass)
    off = -jnp.sqrt(cond / lift(mass))
    b_mat = jnp.where(j8 == r8, diag, jnp.where(j8 == r8 + 1, off, 0.0))
    q_mat = jnp.where(j8 == r8, 1.0, 0.0)
    offsets = {}
    for r in range(1, 8):
        offsets[r] = sorted({((l ^ r) - l) % 8 for l in range(8)})

    def partner(x, r):
        out = None
        lane = j8
        for o in offsets[r]:
            moved = roll(x, -o, 1)
            sel = lax.rem(lane + o, 8) == (lane ^ r)
            out = moved if out is None else jnp.where(sel, moved, out)
        return out

    def sweep(_, carry):
        b, q = carry
        for r in range(1, 8):
            bp, qp = partner(b, r), partner(q, r)
            al = jnp.sum(b * b, axis=0, keepdims=True)
            ap = jnp.sum(bp * bp, axis=0, keepdims=True)
            g = jnp.sum(b * bp, axis=0, keepdims=True)
            d = ap - al
            lane = j8[:1]
            sg = jnp.where(d > 0.0, 2.0, jnp.where(d < 0.0, -2.0, jnp.where(lane < (lane ^ r), 2.0, -2.0)))
            t = sg * g / (jnp.abs(d) + jnp.sqrt(d * d + 4.0 * g * g) + 1e-18)
            c = 1.0 / jnp.sqrt(1.0 + t * t)
            s = c * t
            b, q = c * b - s * bp, c * q - s * qp
        return b, q

    b_mat, q_mat = lax.fori_loop(0, 5, sweep, (b_mat, q_mat))
    lam = jnp.broadcast_to(jnp.sum(b_mat * b_mat, axis=0, keepdims=True), (8, 128))
    root = jnp.sqrt(mass)
    qf = q_mat * root
    qi = q_mat / root
    for j in range(8):
        TF[j * 8 : j * 8 + 8, :] = jnp.broadcast_to(qf[:, j : j + 1], (8, 128))
        TI[j * 8 : j * 8 + 8, :] = jnp.broadcast_to(qi[:, j : j + 1], (8, 128))
        LAM[j] = jnp.broadcast_to(lam[:, j : j + 1], (8, 128))

    for cp in loads[:4]:
        cp.wait()
    lane_c = lanes((YC, 128))

    @pl.loop(0, chunks)
    def _(c):
        y0 = pl.multiple_of(c * YC, YC)
        east = jnp.zeros((YC, 128), f32)
        west = jnp.zeros((YC, 128), f32)
        for k in range(levels):
            o = 16 * k
            rows = pl.ds(y0 + 8, YC)
            wl, wr = W[k, rows, 0:128], W[k, rows, 128:256]
            tl, tr = TH[k, rows, 0:128], TH[k, rows, 128:256]
            ur = U[k, pl.ds(y0, YC), 128:256]
            east = jnp.where((lane_c >= o) & (lane_c < o + 3), roll(wr, o - 125, 1), east)
            east = jnp.where((lane_c >= o + 3) & (lane_c < o + 6), roll(tr, o + 3 - 125, 1), east)
            east = jnp.where(lane_c == o + 6, roll(ur, o + 6 - 127, 1), east)
            west = jnp.where((lane_c >= o) & (lane_c < o + 3), roll(wl, o, 1), west)
            west = jnp.where((lane_c >= o + 3) & (lane_c < o + 6), roll(tl, o + 3, 1), west)
        PE_S[pl.ds(y0, YC), :] = east
        PW_S[pl.ds(y0, YC), :] = west

    for k in range(levels):
        a, b, c = W[k, ny : ny + 8, :], TH[k, ny : ny + 8, :], V[k, ny : ny + 8, :]
        row = rows_of((8, nx))
        YN_S[k] = jnp.where(row < 3, roll(a, 3, 0), jnp.where(row < 6, roll(b, 6, 0), roll(c, 7, 0)))
        a, b = W[k, 8:16, :], TH[k, 8:16, :]
        YS_S[k] = jnp.where(row < 3, a, roll(b, 3, 0))

    pl.semaphore_wait(barrier, nx_dev + ny_dev - 2)
    halos = []
    for i, (src, dst, where) in enumerate(
        [
            (PE_S, PE_R, {"gx": px(1)}),
            (PW_S, PW_R, {"gx": px(nx_dev - 1)}),
            (YN_S, YN_R, {"gy": py(1)}),
            (YS_S, YS_R, {"gy": py(ny_dev - 1)}),
        ]
    ):
        cp = pltpu.make_async_remote_copy(
            src_ref=src, dst_ref=dst, send_sem=hs_sem.at[i], recv_sem=hr_sem.at[i],
            device_id=where, device_id_type=MESH,
        )
        cp.start()
        halos.append(cp)
    for cp in halos:
        cp.wait()

    for k in range(levels):
        n8, s8 = YN_R[k], YS_R[k]
        W[k, 0:8, :] = roll(n8, 5, 0)
        TH[k, 0:8, :] = roll(n8, 2, 0)
        V[k, 0:8, :] = roll(n8, 1, 0)
        W[k, ny + 8 : ny + 16, :] = s8
        TH[k, ny + 8 : ny + 16, :] = roll(s8, 5, 0)

    lane_n = lanes((ny, 128))
    ph, po = PE_R[...], PW_S[...]
    lane_m = lax.rem(lane_n, 16)
    u_th = roll(ph, -3, 1)
    u_top = jnp.where(lane_n >= 112, roll(ph, -6, 1), roll(ph, -22, 1))
    u_w = (roll(ph, -6, 1) + u_top) / 2.0
    FPK[...] = flux(
        ph, roll(ph, -1, 1), roll(ph, -2, 1), po, roll(po, -1, 1), roll(po, -2, 1),
        jnp.where(lane_m == 0, u_w, u_th),
    )

    def nxt(k):
        return min(k + 1, levels - 1)

    def y_shifts(block, n):
        return [roll(block, -s, 0)[8 : 8 + n] if s else block[8 : 8 + n] for s in range(-2, 4)]

    def south_flux(field, first, lifted):
        for k in range(levels):
            block = field[k, 0:16, :]
            qs = [roll(block, -s, 0)[0:8] for s in range(-2, 4)]
            c = V[k, 0:8, :]
            if lifted:
                c = (c + V[nxt(k), 0:8, :]) / 2.0
            FYP[k] = flux(*qs, c)

    def advect(field, k, y0, extra, lifted, fz_below, zi):
        o = 16 * k + extra
        rows = pl.ds(y0 + 8, YC)
        cen = pl.ds(y0, YC)
        block = field[k, pl.ds(y0, YC + 16), :]
        q = block[8 : 8 + YC]
        left, right = q[:, :128], q[:, 128:]
        pe, pw = PW_R[cen, :], PE_R[cen, :]
        ls, rs = [], []
        for s in range(-2, 4):
            if s == 0:
                ls.append(left)
                rs.append(right)
                continue
            a, b = roll(left, -s, 1), roll(right, -s, 1)
            if s > 0:
                ls.append(jnp.where(lane_c < 128 - s, a, b))
                rs.append(jnp.where(lane_c < 128 - s, b, roll(pe, -s - o, 1)))
            else:
                ls.append(jnp.where(lane_c >= -s, a, roll(pw, -s - 3 - o, 1)))
                rs.append(jnp.where(lane_c >= -s, b, a))
        u, v, w = U[k, cen, :], V[k, rows, :], W[k, rows, :]
        if lifted:
            u = (u + U[nxt(k), cen, :]) / 2.0
            v = (v + V[nxt(k), rows, :]) / 2.0
            w = (w + W[nxt(k), rows, :]) / 2.0
        fl = flux(*ls, u[:, :128])
        fr = flux(*rs, u[:, 128:])
        fl_roll = roll(fl, 1, 1)
        wl = jnp.where(lane_c >= 1, fl_roll, roll(FPK[cen, :], -o, 1))
        wr = jnp.where(lane_c >= 1, roll(fr, 1, 1), fl_roll)
        div = jnp.concatenate([fl - wl, fr - wr], axis=1)
        fy = flux(*y_shifts(block, YC), v)
        prev = roll(jnp.concatenate([FYP[k], fy], axis=0), 1, 0)[8:]
        FYP[k] = fy[YC - 8 :]
        div = div + (fy - prev)
        zq = [field[min(max(k + s, 0), levels - 1), rows, :] for s in range(-2, 4)]
        fz = flux(*zq, w)
        tend = (-DT / 60.0) * div - COEF[zi + k : zi + k + 1, :] * fz
        if k > 0:
            tend = tend + COEF[zi + 8 + k : zi + 9 + k, :] * fz_below
        return q, tend, fz

    def send(src, dst, s_sem, r_sem, who):
        return pltpu.make_async_remote_copy(
            src_ref=src, dst_ref=dst, send_sem=s_sem, recv_sem=r_sem,
            device_id=who, device_id_type=MESH,
        )

    south_flux(W, 0, True)

    @pl.loop(0, chunks)
    def _(c):
        y0 = pl.multiple_of(c * YC, YC)
        rows = pl.ds(y0 + 8, YC)
        cen = pl.ds(y0, YC)
        fz, star_below = None, None
        for k in range(levels):
            q, tend, fz = advect(W, k, y0, 0, True, fz, 0)
            star = q + tend + (0.5 * DT) * (TH[k, rows, :] + TH[nxt(k), rows, :])
            WS[k, cen, :] = star
            u = U[k, cen, :]
            ul = roll(u[:, :128], 1, 1)
            uw = jnp.where(lane_c >= 1, ul, roll(PE_R[cen, :], -(16 * k + 6), 1))
            ue = jnp.where(lane_c >= 1, roll(u[:, 128:], 1, 1), ul)
            vb = V[k, pl.ds(y0, YC + 8), :]
            dv = (vb - roll(vb, 1, 0))[8:]
            src = (u - jnp.concatenate([uw, ue], axis=1) + dv) * (1.0 / DT)
            src = src + COEF[32 + k : 33 + k, :] * star
            if k > 0:
                src = src - COEF[40 + k : 41 + k, :] * star_below
            star_below = star
            SRC[k] = src
        for h in range(2):
            hs = slice(128 * h, 128 * h + 128)
            col = [SRC[k, :, hs] for k in range(levels)]
            for j in range(levels):
                acc = TF[j * 8 : j * 8 + 1, :] * col[0]
                for k in range(1, levels):
                    acc = acc + TF[j * 8 + k : j * 8 + k + 1, :] * col[k]
                TX1[j, c, h] = acc
        pltpu.make_async_copy(TX1.at[gx, c], RX1.at[c, gx], l1_sem.at[c]).start()
        for t in range(1, nx_dev):
            g = px(t)
            send(TX1.at[g, c], RX1.at[c, gx], s1_sem.at[c, t], r1_sem.at[c, gx], {"gx": g}).start()

    south_flux(TH, 0, False)

    @pl.loop(0, chunks)
    def _(c):
        y0 = pl.multiple_of(c * YC, YC)
        fz = None
        for k in range(levels):
            q, tend, fz = advect(TH, k, y0, 3, False, fz, 16)
            tn_ref[k, pl.ds(y0, YC), :] = q + tend

    lam_g = LAM[gx]
    rate, scale = [], []
    for h in range(2):
        mu = lam_g + tab_ref[16 + 8 * h : 24 + 8 * h, :]
        rt = jnp.sqrt(mu * mu + 4.0 * mu)
        rate.append(2.0 / (2.0 + mu + rt))
        scale.append(-1.0 / rt)

    loads[4].wait()

    def x_forward(c, carry):
        y0 = pl.multiple_of(c * YC, YC)
        pltpu.make_async_copy(TX1.at[gx, c], RX1.at[c, gx], l1_sem.at[c]).wait()
        for t in range(1, nx_dev):
            g = px(t)
            send(TX1.at[g, c], RX1.at[c, g], s1_sem.at[c, t], r1_sem.at[c, g], {"gx": g}).wait_recv()
        for i in range(YC // 8):
            sub = slice(8 * i, 8 * i + 8)
            x = [RX1[c, q // 2, q % 2, sub, :] for q in range(16)]
            y_0, y_8, re, im = fwd16(x)
            Z[8 * i : 8 * i + 8, 0:128] = y_0
            Z[8 * i : 8 * i + 8, 128:256] = y_8
            for m in range(1, 8):
                co, si = tab_ref[m : m + 1, :], tab_ref[8 + m : 9 + m, :]
                at = m * YC + 8 * i
                Z[at : at + 8, 0:128] = re[m] * co + im[m] * si
                Z[at : at + 8, 128:256] = im[m] * co - re[m] * si
        o0 = dot3(Z[0:YC, :], MATS[2], MATS[3])
        om = dot3(Z[YC : 8 * YC, :], MATS[0], MATS[1])
        for m in range(8):
            val = o0 if m == 0 else om[(m - 1) * YC : m * YC]
            for h in range(2):
                S[h, pl.ds(y0 * 8 + m, YC, stride=8), :] = val[:, 128 * h : 128 * h + 128]
        a0, a1, b0, b1, p0, p1 = carry
        for i in range(YC):
            f0 = S[0, pl.ds(y0 * 8 + 8 * i, 8), :]
            f1 = S[1, pl.ds(y0 * 8 + 8 * i, 8), :]
            a0, a1 = f0 + rate[0] * a0, f1 + rate[1] * a1
            b0, b1 = b0 + p0 * f0, b1 + p1 * f1
            p0, p1 = p0 * rate[0], p1 * rate[1]
        return a0, a1, b0, b1, p0, p1

    zero = jnp.zeros((8, 128), f32)
    one = jnp.ones((8, 128), f32)
    a0, a1, b0, b1, p0, p1 = lax.fori_loop(0, chunks, x_forward, (zero, zero, zero, zero, one, one))

    half = 16
    for h, (a, b, p) in enumerate([(a0, b0, p0), (a1, b1, p1)]):
        for j in range(8):
            IFS[h * 8 + j] = a[j : j + 1, :]
            IFS[half + h * 8 + j] = b[j : j + 1, :]
            RP[h * 8 + j] = p[j : j + 1, :]
    IFR[0] = IFS[gy]

    @pl.loop(1, ny_dev)
    def _(t):
        i = py(t)
        slot = (ny_dev - t) + (i // half) * (2 * t - ny_dev)
        send(IFS.at[i], IFR.at[slot], is_sem.at[0], ir_sem.at[0], {"gy": i}).start()

    others = pl.ds(1, ny_dev - 1)
    send(IFS.at[others], IFR.at[others], is_sem.at[0], ir_sem.at[0], {"gy": py(1)}).wait()
    acc = IFR[...]
    power = RP[lax.rem(gy, half)][None]
    step = 1
    while step < ny_dev:
        acc = acc + power * jnp.concatenate([acc[ny_dev - step :], acc[: ny_dev - step]], axis=0)
        power = power * power
        step *= 2
    acc = acc * (1.0 / (1.0 - power))
    IFO[...] = jnp.concatenate([acc[ny_dev - 1 :], acc[: ny_dev - 1]], axis=0)
    IFB[gy] = IFO[0]
    sign = 1 - 2 * (gy // half)

    @pl.loop(1, ny_dev)
    def _(t):
        dev = lax.rem(gy + t * sign + ny_dev, ny_dev)
        send(IFO.at[t], IFB.at[gy], is_sem.at[1], ir_sem.at[1], {"gy": dev}).start()

    send(IFO.at[others], IFB.at[others], is_sem.at[1], ir_sem.at[1], {"gy": py(1)}).wait()
    ain = [jnp.concatenate([IFB[h * 8 + j] for j in range(8)], axis=0) for h in range(2)]
    bin_ = [jnp.concatenate([IFB[half + h * 8 + j] for j in range(8)], axis=0) for h in range(2)]

    def back(i, carry):
        y = ny - 1 - i
        at = pl.ds(pl.multiple_of(y * 8, 8), 8)
        out = []
        for h in range(2):
            b = S[h, at, :] + rate[h] * carry[h]
            SB[h, at, :] = rate[h] * carry[h]
            out.append(b)
        return tuple(out)

    lax.fori_loop(0, ny, back, tuple(bin_), unroll=8)

    def forth(y, carry):
        at = pl.ds(pl.multiple_of(y * 8, 8), 8)
        out = []
        for h in range(2):
            a = S[h, at, :] + rate[h] * carry[h]
            S[h, at, :] = scale[h] * (a + SB[h, at, :])
            out.append(a)
        return tuple(out)

    last = lax.fori_loop(0, ny, forth, tuple(ain), unroll=8)
    for h in range(2):
        S[h, ny * 8 : ny * 8 + 8, :] = scale[h] * (rate[h] * last[h] + bin_[h])
        S[h, ny * 8 + 8 : ny * 8 + 64, :] = jnp.zeros((56, 128), f32)

    def x_inverse(y0, n, put):
        for m in range(8):
            for h in range(2):
                Z[m * n : m * n + n, 128 * h : 128 * h + 128] = S[h, pl.ds(y0 * 8 + m, n, stride=8), :]
        o0 = dot3(Z[0:n, :], MATS[6], MATS[7])
        om = dot3(Z[n : 8 * n, :], MATS[4], MATS[5])
        Z[0:n, :] = o0
        Z[n : 8 * n, :] = om
        for i in range(n // 8):
            zr, zi = {}, {}
            for m in range(1, 8):
                co, si = tab_ref[m : m + 1, :], tab_ref[8 + m : 9 + m, :]
                at = m * n + 8 * i
                a, b = Z[at : at + 8, 0:128], Z[at : at + 8, 128:256]
                zr[m] = a * co - b * si
                zi[m] = a * si + b * co
            put(i, inv16(Z[8 * i : 8 * i + 8, 0:128], Z[8 * i : 8 * i + 8, 128:256], zr, zi))

    lane_8 = lanes((8, 128))

    @pl.loop(0, chunks)
    def _(c):
        y0 = pl.multiple_of(c * YC, YC)

        def put(i, x):
            edge = jnp.zeros((8, 128), f32)
            for q in range(16):
                TX2[q // 2, c, q % 2, 8 * i : 8 * i + 8, :] = x[q]
            for d in range(nx_dev):
                edge = jnp.where(lane_8 == d, roll(x[(2 * d + 2) % 16], d, 1), edge)
            EW[pl.ds(y0 + 8 * i, 8), :] = edge

        x_inverse(y0, YC, put)
        pltpu.make_async_copy(TX2.at[gx, c], RX2.at[c, gx], l2_sem.at[c]).start()
        for t in range(1, nx_dev):
            g = px(t)
            send(TX2.at[g, c], RX2.at[c, gx], s2_sem.at[c, t], r2_sem.at[c, gx], {"gx": g}).start()

    EW[ny:128, :] = jnp.zeros((128 - ny, 128), f32)
    ewt = jnp.transpose(EW[...])
    row8 = rows_of((8, 128))

    def put_north(i, x):
        for d in range(nx_dev):
            e = jnp.broadcast_to(ewt[d : d + 1, :], (8, 128))
            n0 = jnp.broadcast_to(x[2 * d][0:1], (8, 128))
            n1 = jnp.broadcast_to(x[2 * d + 1][0:1], (8, 128))
            X2[d] = jnp.where(row8 == 0, n0, jnp.where(row8 == 1, n1, e))

    x_inverse(ny, 8, put_north)
    pltpu.make_async_copy(X2.at[gx], XR.at[gx], l2_sem.at[chunks]).start()
    for t in range(1, nx_dev):
        g = px(t)
        send(X2.at[g], XR.at[gx], sx_sem.at[t], rx_sem.at[gx], {"gx": g}).start()

    @pl.loop(0, chunks)
    def _(c):
        cen = pl.ds(pl.multiple_of(c * YC, YC), YC)
        pltpu.make_async_copy(TX2.at[gx, c], RX2.at[c, gx], l2_sem.at[c]).wait()
        for t in range(1, nx_dev):
            g = px(t)
            send(TX2.at[g, c], RX2.at[c, g], s2_sem.at[c, t], r2_sem.at[c, g], {"gx": g}).wait_recv()
        for h in range(2):
            col = [RX2[c, j, h] for j in range(levels)]
            for k in range(levels):
                acc = TI[k : k + 1, :] * col[0]
                for j in range(1, levels):
                    acc = acc + TI[j * 8 + k : j * 8 + k + 1, :] * col[j]
                p_ref[k, cen, 128 * h : 128 * h + 128] = acc

    pltpu.make_async_copy(X2.at[gx], XR.at[gx], l2_sem.at[chunks]).wait()
    for t in range(1, nx_dev):
        g = px(t)
        send(X2.at[g], XR.at[g], sx_sem.at[t], rx_sem.at[g], {"gx": g}).wait_recv()
    east = jnp.zeros((8, 128), f32)
    for k in range(levels):
        acc = TI[k : k + 1, :] * XR[0]
        for j in range(1, levels):
            acc = acc + TI[j * 8 + k : j * 8 + k + 1, :] * XR[j]
        EX[k] = acc
        east = jnp.where(row8 == k, jnp.broadcast_to(acc[2:3, :], (8, 128)), east)
    EC[0:8, :] = east
    EC[8:128, :] = jnp.zeros((120, 128), f32)
    EC[...] = jnp.transpose(EC[...])

    @pl.loop(0, levels)
    def _(k):
        p = p_ref[k]
        pleft, pright = p[:, :128], p[:, 128:]
        ec = EC[0:ny, :]
        col = jnp.sum(jnp.where(lane_n == k, ec, 0.0), axis=1, keepdims=True)
        a, b = roll(pleft, -1, 1), roll(pright, -1, 1)
        gl = jnp.where(lane_n < 127, a, b) - pleft
        gr = jnp.where(lane_n < 127, b, jnp.broadcast_to(col, (ny, 128))) - pright
        un_ref[k] = U[k] - DT * jnp.concatenate([gl, gr], axis=1)
        ex = EX[k]
        north = jnp.concatenate([ex[0:1, :], ex[1:2, :]], axis=1)
        shifted = roll(p, -1, 0)
        shifted = jnp.where(rows_of((ny, nx)) < ny - 1, shifted, jnp.broadcast_to(north, (ny, nx)))
        vn_ref[k] = V[k, mid, :] - DT * (shifted - p)

    for k in range(levels):
        g = COEF[48 + k : 49 + k, :]
        if k + 1 < levels:
            wn_ref[k] = WS[k] - g * (p_ref[k + 1] - p_ref[k])
        else:
            wn_ref[k] = WS[k] + g * p_ref[k]

    @pl.loop(0, chunks)
    def _(c):
        for t in range(1, nx_dev):
            g = px(t)
            send(TX1.at[g, c], RX1.at[c, g], s1_sem.at[c, t], r1_sem.at[c, g], {"gx": g}).wait_send()
            send(TX2.at[g, c], RX2.at[c, g], s2_sem.at[c, t], r2_sem.at[c, g], {"gx": g}).wait_send()

    for t in range(1, nx_dev):
        g = px(t)
        send(X2.at[g], XR.at[g], sx_sem.at[t], rx_sem.at[g], {"gx": g}).wait_send()


def per_device(u_face, v_face, w_face, theta_field, density, thickness):
    nx_dev = lax.axis_size("gx")
    ny_dev = lax.axis_size("gy")
    levels, ny, nx = u_face.shape
    chunks = ny // YC
    mats, tab = tables()
    vm = pltpu.VMEM
    dma = pltpu.SemaphoreType.DMA
    out = jax.ShapeDtypeStruct(u_face.shape, f32)
    any_ = pl.BlockSpec(memory_space=pl.ANY)
    smem = pl.BlockSpec(memory_space=pltpu.SMEM)
    vmem = pl.BlockSpec(memory_space=pltpu.VMEM)
    scratch = [
        vm((levels, ny, nx), f32),
        vm((levels, ny + 8, nx), f32),
        vm((levels, ny + 16, nx), f32),
        vm((levels, ny + 16, nx), f32),
        vm((8, 256, 256), bf16),
        vm((56, 256), f32),
        vm((64, 128), f32),
        vm((64, 128), f32),
        vm((8, 8, 128), f32),
        vm((ny, 128), f32), vm((ny, 128), f32), vm((ny, 128), f32), vm((ny, 128), f32),
        vm((levels, 8, nx), f32), vm((levels, 8, nx), f32),
        vm((levels, 8, nx), f32), vm((levels, 8, nx), f32),
        vm((ny, 128), f32),
        vm((levels, 8, nx), f32),
        vm((levels, ny, nx), f32),
        vm((levels, YC, nx), f32),
        vm((levels, chunks, 2, YC, 128), f32),
        vm((chunks, nx_dev, 2, YC, 128), f32),
        vm((8 * YC, 256), f32),
        vm((2, (ny + 8) * 8, 128), f32),
        vm((2, ny * 8, 128), f32),
        vm((32, 1, 128), f32), vm((32, 1, 128), f32), vm((32, 1, 128), f32), vm((32, 1, 128), f32),
        vm((16, 1, 128), f32),
        vm((nx_dev, chunks, 2, YC, 128), f32),
        vm((chunks, levels, 2, YC, 128), f32),
        vm((nx_dev, 8, 128), f32),
        vm((levels, 8, 128), f32),
        vm((128, 128), f32),
        vm((128, 128), f32),
        vm((levels, 8, 128), f32),
        dma((5,)), dma((4,)), dma((4,)),
        dma((chunks, nx_dev)), dma((chunks, nx_dev)), dma((chunks,)),
        dma((2,)), dma((2,)),
        dma((chunks, nx_dev)), dma((chunks, nx_dev)), dma((chunks + 1,)),
        dma((nx_dev,)), dma((nx_dev,)),
    ]
    return pl.pallas_call(
        functools.partial(kernel, nx_dev, ny_dev),
        out_shape=(out,) * 5,
        in_specs=[smem, smem, vmem, any_, any_, any_, any_, any_],
        out_specs=(vmem,) * 5,
        scratch_shapes=scratch,
        compiler_params=pltpu.CompilerParams(
            collective_id=0, has_side_effects=True, vmem_limit_bytes=40 << 20
        ),
        name="substep",
    )(density, thickness, jnp.asarray(tab), u_face, v_face, w_face, theta_field, jnp.asarray(mats))


def solution(mesh):
    spec = P(None, "gy", "gx")
    return jax.shard_map(
        per_device,
        mesh=mesh,
        in_specs=(spec, spec, spec, spec, P(), P()),
        out_specs=(spec,) * 5,
        check_vma=False,
    )
```

```python
import functools

import jax
import jax.numpy as jnp
import numpy as np
from jax import lax
from jax.experimental import pallas as pl
from jax.experimental.pallas import tpu as pltpu
from jax.sharding import PartitionSpec as P

DT = 0.2
f32 = jnp.float32
bf16 = jnp.bfloat16
MESH = pl.DeviceIdType.MESH
C1, C2, C3 = float(np.cos(np.pi / 8)), float(np.cos(np.pi / 4)), float(np.cos(3 * np.pi / 8))
YC = 16


def split_bf16(a):
    hi = a.astype(jnp.bfloat16)
    lo = (a - hi.astype(np.float64)).astype(jnp.bfloat16)
    return hi, lo


@functools.cache
def tables():
    n_x = 2048
    l = np.arange(128)
    n = np.arange(128)

    def cas(t):
        return np.cos(t) + np.sin(t)

    cos = np.cos(2 * np.pi * np.outer(l, n) / 128)
    sin = np.sin(2 * np.pi * np.outer(l, n) / 128)
    zero = np.zeros((128, 128))
    fw = np.block([[cos, -sin], [sin, cos]])
    b0 = cas(2 * np.pi * np.outer(l, n) / 128)
    b8 = cas(2 * np.pi * np.outer(l, 16 * n + 8) / n_x)
    fb = np.block([[b0, zero], [zero, b8]])
    mats = []
    for m in (fw, fb, fw.T * (2 / n_x), fb.T * (1 / n_x)):
        mats.extend(split_bf16(m))
    mats = np.stack(mats)
    tw = np.arange(8)[:, None] * l[None, :] * (2 * np.pi / n_x)
    k_lo = 16 * n[None, :] + np.arange(8)[:, None]
    k_hi = k_lo.copy()
    k_hi[0] += 8
    tab = np.concatenate(
        [np.cos(tw), np.sin(tw), 4 * np.sin(np.pi * k_lo / n_x) ** 2, 4 * np.sin(np.pi * k_hi / n_x) ** 2]
    ).astype(np.float32)
    return mats, tab


def fwd16(x):
    s = [x[q] + x[q + 8] for q in range(8)]
    d = [x[q] - x[q + 8] for q in range(8)]
    t = [s[q] + s[q + 4] for q in range(4)]
    e = [s[q] - s[q + 4] for q in range(4)]
    t02, t13 = t[0] + t[2], t[1] + t[3]
    re, im = {}, {}
    y0, y8 = t02 + t13, t02 - t13
    re[4], im[4] = t[0] - t[2], t[3] - t[1]
    a, b = C2 * (e[1] - e[3]), C2 * (e[1] + e[3])
    re[2], re[6] = e[0] + a, e[0] - a
    im[2], im[6] = -(e[2] + b), e[2] - b
    u = [None] + [d[q] - d[8 - q] for q in (1, 2, 3)]
    v = [None] + [d[q] + d[8 - q] for q in (1, 2, 3)]
    g = C2 * u[2]
    g1, g2 = d[0] + g, d[0] - g
    h1, h2 = C1 * u[1] + C3 * u[3], C3 * u[1] - C1 * u[3]
    re[1], re[7], re[3], re[5] = g1 + h1, g1 - h1, g2 + h2, g2 - h2
    k = C2 * v[2]
    k1, k2 = k + d[4], k - d[4]
    m1, m2 = C3 * v[1] + C1 * v[3], C1 * v[1] - C3 * v[3]
    im[1], im[7], im[3], im[5] = -(m1 + k1), k1 - m1, -(m2 + k2), k2 - m2
    return y0, y8, re, im


def inv16(a0, a8, zr, zi):
    p1, m1, p3, m3 = zr[1] + zr[7], zr[1] - zr[7], zr[3] + zr[5], zr[3] - zr[5]
    r1, s1, r3, s3 = zi[1] + zi[7], zi[1] - zi[7], zi[3] + zi[5], zi[3] - zi[5]
    o = [None] * 8
    o[0] = p1 + p3
    o[4] = s3 - s1
    cs = [None, C1 * m1 + C3 * m3, C2 * (p1 - p3), C3 * m1 - C1 * m3]
    sn = [None, C3 * r1 + C1 * r3, C2 * (s1 + s3), C1 * r1 - C3 * r3]
    for q in (1, 2, 3):
        o[q] = cs[q] - sn[q]
        o[8 - q] = -cs[q] - sn[q]
    ap, am = a0 + a8, a0 - a8
    g = [ap + zr[4], am - zi[4], ap - zr[4], am + zi[4]]
    w1, w2 = C2 * (zr[2] - zr[6]), C2 * (zi[2] + zi[6])
    h = [zr[2] + zr[6], w1 - w2, zi[6] - zi[2], -w1 - w2]
    ev = [g[q] + h[q] for q in range(4)] + [g[q] - h[q] for q in range(4)]
    return [ev[q] + o[q] for q in range(8)] + [ev[q] - o[q] for q in range(8)]


def dot3(x, hi, lo):
    xh = x.astype(bf16)
    xl = (x - xh.astype(f32)).astype(bf16)
    out = jnp.dot(xh, hi, preferred_element_type=f32)
    out += jnp.dot(xl, hi, preferred_element_type=f32)
    out += jnp.dot(xh, lo, preferred_element_type=f32)
    return out


def flux(qm2, qm1, q0, q1, q2, q3, c):
    s = 37.0 * (q0 + q1) - 8.0 * (qm1 + q2) + (qm2 + q3)
    d = 10.0 * (q1 - q0) - 5.0 * (q2 - qm1) + (q3 - qm2)
    return c * s - jnp.abs(c) * d


def roll(x, shift, axis):
    n = x.shape[axis]
    shift = shift % n
    return x if shift == 0 else pltpu.roll(x, shift, axis)


def lanes(shape):
    return lax.broadcasted_iota(jnp.int32, shape, len(shape) - 1)


def rows_of(shape):
    return lax.broadcasted_iota(jnp.int32, shape, 0)


def kernel(
    nx_dev, ny_dev,
    den_hbm, thk_hbm, tab_hbm, u_hbm, v_hbm, w_hbm, th_hbm, mats_hbm,
    U, V, WS, tn_ref, RX2, XR, TI, COEF,
    den_ref, thk_ref, tab_ref, W, TH, MATS, TF, LAM,
    PE_S, PW_S, PE_R, PW_R, YN_S, YS_S, YN_R, YS_R, FPK, FYP,
    SRC, TX1, RX1, Z, S, SB, IFS, IFR, IFO, IFB, RP, TX2, X2, EW,
    in_sem, hs_sem, hr_sem, s1_sem, r1_sem, l1_sem, is_sem, ir_sem, s2_sem, r2_sem, l2_sem,
    sx_sem, rx_sem,
):
    gx = lax.axis_index("gx")
    gy = lax.axis_index("gy")
    levels, ny, nx = u_hbm.shape
    chunks = ny // YC

    def px(t):
        return lax.rem(gx + t, nx_dev)

    def py(t):
        return lax.rem(gy + t, ny_dev)

    mid = pl.ds(8, ny)
    small = [
        pltpu.make_async_copy(den_hbm, den_ref, in_sem.at[5]),
        pltpu.make_async_copy(thk_hbm, thk_ref, in_sem.at[6]),
        pltpu.make_async_copy(tab_hbm, tab_ref, in_sem.at[7]),
    ]
    loads = [
        pltpu.make_async_copy(w_hbm, W.at[:, mid, :], in_sem.at[0]),
        pltpu.make_async_copy(th_hbm, TH.at[:, mid, :], in_sem.at[1]),
        pltpu.make_async_copy(u_hbm, U, in_sem.at[2]),
        pltpu.make_async_copy(v_hbm, V.at[:, mid, :], in_sem.at[3]),
        pltpu.make_async_copy(mats_hbm, MATS, in_sem.at[4]),
    ]
    for cp in small + loads:
        cp.start()

    barrier = pltpu.get_barrier_semaphore()
    for t in range(1, nx_dev):
        pl.semaphore_signal(barrier, inc=1, device_id={"gx": px(t)}, device_id_type=MESH)

    @pl.loop(1, ny_dev)
    def _(t):
        pl.semaphore_signal(barrier, inc=1, device_id={"gy": py(t)}, device_id_type=MESH)

    for cp in small:
        cp.wait()

    r8 = rows_of((8, 128))
    j8 = lax.rem(lanes((8, 128)), 8)
    den = jnp.zeros((8, 128), f32)
    thk = jnp.zeros((8, 128), f32)
    for k in range(levels):
        den = jnp.where(r8 == k, den_ref[k], den)
        thk = jnp.where(r8 == k, thk_ref[k], thk)

    def lift(a):
        return jnp.where(r8 == 7, a, roll(a, -1, 0))

    def below(a):
        return jnp.where(r8 == 0, 0.0, roll(a, 1, 0))

    lden = lift(den)
    fd = (den + lden) / 2.0
    fs = (thk + lift(thk)) / 2.0
    mass = den * thk
    zw = (DT / 60.0) / (fd * fs)
    zt = (DT / 60.0) / mass
    sc = (1.0 / DT) / mass
    coefs = [lden * zw, below(lden) * zw, fd * zt, below(fd) * zt, fd * sc, below(fd) * sc, DT / fs]
    for i, a in enumerate(coefs):
        COEF[i * 8 : i * 8 + 8, :] = jnp.concatenate([a, a], axis=1)

    cond = fd / fs
    diag = jnp.sqrt(cond / mass)
    off = -jnp.sqrt(cond / lift(mass))
    b_mat = jnp.where(j8 == r8, diag, jnp.where(j8 == r8 + 1, off, 0.0))
    q_mat = jnp.where(j8 == r8, 1.0, 0.0)
    offsets = {}
    for r in range(1, 8):
        offsets[r] = sorted({((l ^ r) - l) % 8 for l in range(8)})

    def partner(x, r):
        out = None
        lane = j8
        for o in offsets[r]:
            moved = roll(x, -o, 1)
            sel = lax.rem(lane + o, 8) == (lane ^ r)
            out = moved if out is None else jnp.where(sel, moved, out)
        return out

    def sweep(_, carry):
        b, q = carry
        for r in range(1, 8):
            bp, qp = partner(b, r), partner(q, r)
            al = jnp.sum(b * b, axis=0, keepdims=True)
            ap = jnp.sum(bp * bp, axis=0, keepdims=True)
            g = jnp.sum(b * bp, axis=0, keepdims=True)
            d = ap - al
            lane = j8[:1]
            sg = jnp.where(d > 0.0, 2.0, jnp.where(d < 0.0, -2.0, jnp.where(lane < (lane ^ r), 2.0, -2.0)))
            t = sg * g / (jnp.abs(d) + jnp.sqrt(d * d + 4.0 * g * g) + 1e-18)
            c = 1.0 / jnp.sqrt(1.0 + t * t)
            s = c * t
            b, q = c * b - s * bp, c * q - s * qp
        return b, q

    b_mat, q_mat = lax.fori_loop(0, 5, sweep, (b_mat, q_mat))
    lam = jnp.broadcast_to(jnp.sum(b_mat * b_mat, axis=0, keepdims=True), (8, 128))
    root = jnp.sqrt(mass)
    qf = q_mat * root
    qi = q_mat / root
    for j in range(8):
        TF[j * 8 : j * 8 + 8, :] = jnp.broadcast_to(qf[:, j : j + 1], (8, 128))
        TI[j * 8 : j * 8 + 8, :] = jnp.broadcast_to(qi[:, j : j + 1], (8, 128))
        LAM[j] = jnp.broadcast_to(lam[:, j : j + 1], (8, 128))

    for cp in loads[:4]:
        cp.wait()
    lane_c = lanes((YC, 128))

    @pl.loop(0, chunks)
    def _(c):
        y0 = pl.multiple_of(c * YC, YC)
        east = jnp.zeros((YC, 128), f32)
        west = jnp.zeros((YC, 128), f32)
        for k in range(levels):
            o = 16 * k
            rows = pl.ds(y0 + 8, YC)
            wl, wr = W[k, rows, 0:128], W[k, rows, 128:256]
            tl, tr = TH[k, rows, 0:128], TH[k, rows, 128:256]
            ur = U[k, pl.ds(y0, YC), 128:256]
            east = jnp.where((lane_c >= o) & (lane_c < o + 3), roll(wr, o - 125, 1), east)
            east = jnp.where((lane_c >= o + 3) & (lane_c < o + 6), roll(tr, o + 3 - 125, 1), east)
            east = jnp.where(lane_c == o + 6, roll(ur, o + 6 - 127, 1), east)
            west = jnp.where((lane_c >= o) & (lane_c < o + 3), roll(wl, o, 1), west)
            west = jnp.where((lane_c >= o + 3) & (lane_c < o + 6), roll(tl, o + 3, 1), west)
        PE_S[pl.ds(y0, YC), :] = east
        PW_S[pl.ds(y0, YC), :] = west

    for k in range(levels):
        a, b, c = W[k, ny : ny + 8, :], TH[k, ny : ny + 8, :], V[k, ny : ny + 8, :]
        row = rows_of((8, nx))
        YN_S[k] = jnp.where(row < 3, roll(a, 3, 0), jnp.where(row < 6, roll(b, 6, 0), roll(c, 7, 0)))
        a, b = W[k, 8:16, :], TH[k, 8:16, :]
        YS_S[k] = jnp.where(row < 3, a, roll(b, 3, 0))

    pl.semaphore_wait(barrier, nx_dev + ny_dev - 2)
    halos = []
    for i, (src, dst, where) in enumerate(
        [
            (PE_S, PE_R, {"gx": px(1)}),
            (PW_S, PW_R, {"gx": px(nx_dev - 1)}),
            (YN_S, YN_R, {"gy": py(1)}),
            (YS_S, YS_R, {"gy": py(ny_dev - 1)}),
        ]
    ):
        cp = pltpu.make_async_remote_copy(
            src_ref=src, dst_ref=dst, send_sem=hs_sem.at[i], recv_sem=hr_sem.at[i],
            device_id=where, device_id_type=MESH,
        )
        cp.start()
        halos.append(cp)
    for cp in halos:
        cp.wait()

    for k in range(levels):
        n8, s8 = YN_R[k], YS_R[k]
        W[k, 0:8, :] = roll(n8, 5, 0)
        TH[k, 0:8, :] = roll(n8, 2, 0)
        V[k, 0:8, :] = roll(n8, 1, 0)
        W[k, ny + 8 : ny + 16, :] = s8
        TH[k, ny + 8 : ny + 16, :] = roll(s8, 5, 0)

    lane_n = lanes((ny, 128))
    ph, po = PE_R[...], PW_S[...]
    lane_m = lax.rem(lane_n, 16)
    u_th = roll(ph, -3, 1)
    u_top = jnp.where(lane_n >= 112, roll(ph, -6, 1), roll(ph, -22, 1))
    u_w = (roll(ph, -6, 1) + u_top) / 2.0
    FPK[...] = flux(
        ph, roll(ph, -1, 1), roll(ph, -2, 1), po, roll(po, -1, 1), roll(po, -2, 1),
        jnp.where(lane_m == 0, u_w, u_th),
    )

    def nxt(k):
        return min(k + 1, levels - 1)

    def y_shifts(block, n):
        return [roll(block, -s, 0)[8 : 8 + n] if s else block[8 : 8 + n] for s in range(-2, 4)]

    def south_flux(field, first, lifted):
        for k in range(levels):
            block = field[k, 0:16, :]
            qs = [roll(block, -s, 0)[0:8] for s in range(-2, 4)]
            c = V[k, 0:8, :]
            if lifted:
                c = (c + V[nxt(k), 0:8, :]) / 2.0
            FYP[k] = flux(*qs, c)

    def advect(field, k, y0, extra, lifted, fz_below, zi):
        o = 16 * k + extra
        rows = pl.ds(y0 + 8, YC)
        cen = pl.ds(y0, YC)
        block = field[k, pl.ds(y0, YC + 16), :]
        q = block[8 : 8 + YC]
        left, right = q[:, :128], q[:, 128:]
        pe, pw = PW_R[cen, :], PE_R[cen, :]
        ls, rs = [], []
        for s in range(-2, 4):
            if s == 0:
                ls.append(left)
                rs.append(right)
                continue
            a, b = roll(left, -s, 1), roll(right, -s, 1)
            if s > 0:
                ls.append(jnp.where(lane_c < 128 - s, a, b))
                rs.append(jnp.where(lane_c < 128 - s, b, roll(pe, -s - o, 1)))
            else:
                ls.append(jnp.where(lane_c >= -s, a, roll(pw, -s - 3 - o, 1)))
                rs.append(jnp.where(lane_c >= -s, b, a))
        u, v, w = U[k, cen, :], V[k, rows, :], W[k, rows, :]
        if lifted:
            u = (u + U[nxt(k), cen, :]) / 2.0
            v = (v + V[nxt(k), rows, :]) / 2.0
            w = (w + W[nxt(k), rows, :]) / 2.0
        fl = flux(*ls, u[:, :128])
        fr = flux(*rs, u[:, 128:])
        fl_roll = roll(fl, 1, 1)
        wl = jnp.where(lane_c >= 1, fl_roll, roll(FPK[cen, :], -o, 1))
        wr = jnp.where(lane_c >= 1, roll(fr, 1, 1), fl_roll)
        div = jnp.concatenate([fl - wl, fr - wr], axis=1)
        fy = flux(*y_shifts(block, YC), v)
        prev = roll(jnp.concatenate([FYP[k], fy], axis=0), 1, 0)[8:]
        FYP[k] = fy[YC - 8 :]
        div = div + (fy - prev)
        zq = [field[min(max(k + s, 0), levels - 1), rows, :] for s in range(-2, 4)]
        fz = flux(*zq, w)
        tend = (-DT / 60.0) * div - COEF[zi + k : zi + k + 1, :] * fz
        if k > 0:
            tend = tend + COEF[zi + 8 + k : zi + 9 + k, :] * fz_below
        return q, tend, fz

    def send(src, dst, s_sem, r_sem, who):
        return pltpu.make_async_remote_copy(
            src_ref=src, dst_ref=dst, send_sem=s_sem, recv_sem=r_sem,
            device_id=who, device_id_type=MESH,
        )

    south_flux(W, 0, True)

    @pl.loop(0, chunks)
    def _(c):
        y0 = pl.multiple_of(c * YC, YC)
        rows = pl.ds(y0 + 8, YC)
        cen = pl.ds(y0, YC)
        fz, star_below = None, None
        for k in range(levels):
            q, tend, fz = advect(W, k, y0, 0, True, fz, 0)
            star = q + tend + (0.5 * DT) * (TH[k, rows, :] + TH[nxt(k), rows, :])
            WS[k, cen, :] = star
            u = U[k, cen, :]
            ul = roll(u[:, :128], 1, 1)
            uw = jnp.where(lane_c >= 1, ul, roll(PE_R[cen, :], -(16 * k + 6), 1))
            ue = jnp.where(lane_c >= 1, roll(u[:, 128:], 1, 1), ul)
            vb = V[k, pl.ds(y0, YC + 8), :]
            dv = (vb - roll(vb, 1, 0))[8:]
            src = (u - jnp.concatenate([uw, ue], axis=1) + dv) * (1.0 / DT)
            src = src + COEF[32 + k : 33 + k, :] * star
            if k > 0:
                src = src - COEF[40 + k : 41 + k, :] * star_below
            star_below = star
            SRC[k] = src
        for h in range(2):
            hs = slice(128 * h, 128 * h + 128)
            col = [SRC[k, :, hs] for k in range(levels)]
            for j in range(levels):
                acc = TF[j * 8 : j * 8 + 1, :] * col[0]
                for k in range(1, levels):
                    acc = acc + TF[j * 8 + k : j * 8 + k + 1, :] * col[k]
                TX1[j, c, h] = acc
        pltpu.make_async_copy(TX1.at[gx, c], RX1.at[c, gx], l1_sem.at[c]).start()
        for t in range(1, nx_dev):
            g = px(t)
            send(TX1.at[g, c], RX1.at[c, gx], s1_sem.at[c, t], r1_sem.at[c, gx], {"gx": g}).start()

    south_flux(TH, 0, False)

    @pl.loop(0, chunks)
    def _(c):
        y0 = pl.multiple_of(c * YC, YC)
        fz = None
        for k in range(levels):
            q, tend, fz = advect(TH, k, y0, 3, False, fz, 16)
            tn_ref[k, pl.ds(y0, YC), :] = q + tend

    lam_g = LAM[gx]
    rate, scale = [], []
    for h in range(2):
        mu = lam_g + tab_ref[16 + 8 * h : 24 + 8 * h, :]
        rt = jnp.sqrt(mu * mu + 4.0 * mu)
        rate.append(2.0 / (2.0 + mu + rt))
        scale.append(-1.0 / rt)

    loads[4].wait()

    def x_forward(c, carry):
        y0 = pl.multiple_of(c * YC, YC)
        pltpu.make_async_copy(TX1.at[gx, c], RX1.at[c, gx], l1_sem.at[c]).wait()
        for t in range(1, nx_dev):
            g = px(t)
            send(TX1.at[g, c], RX1.at[c, g], s1_sem.at[c, t], r1_sem.at[c, g], {"gx": g}).wait_recv()
        for i in range(YC // 8):
            sub = slice(8 * i, 8 * i + 8)
            x = [RX1[c, q // 2, q % 2, sub, :] for q in range(16)]
            y_0, y_8, re, im = fwd16(x)
            Z[8 * i : 8 * i + 8, 0:128] = y_0
            Z[8 * i : 8 * i + 8, 128:256] = y_8
            for m in range(1, 8):
                co, si = tab_ref[m : m + 1, :], tab_ref[8 + m : 9 + m, :]
                at = m * YC + 8 * i
                Z[at : at + 8, 0:128] = re[m] * co + im[m] * si
                Z[at : at + 8, 128:256] = im[m] * co - re[m] * si
        o0 = dot3(Z[0:YC, :], MATS[2], MATS[3])
        om = dot3(Z[YC : 8 * YC, :], MATS[0], MATS[1])
        for m in range(8):
            val = o0 if m == 0 else om[(m - 1) * YC : m * YC]
            for h in range(2):
                S[h, pl.ds(y0 * 8 + m, YC, stride=8), :] = val[:, 128 * h : 128 * h + 128]
        a0, a1, b0, b1, p0, p1 = carry
        for i in range(YC):
            f0 = S[0, pl.ds(y0 * 8 + 8 * i, 8), :]
            f1 = S[1, pl.ds(y0 * 8 + 8 * i, 8), :]
            a0, a1 = f0 + rate[0] * a0, f1 + rate[1] * a1
            b0, b1 = b0 + p0 * f0, b1 + p1 * f1
            p0, p1 = p0 * rate[0], p1 * rate[1]
        return a0, a1, b0, b1, p0, p1

    zero = jnp.zeros((8, 128), f32)
    one = jnp.ones((8, 128), f32)
    a0, a1, b0, b1, p0, p1 = lax.fori_loop(0, chunks, x_forward, (zero, zero, zero, zero, one, one))

    half = 16
    for h, (a, b, p) in enumerate([(a0, b0, p0), (a1, b1, p1)]):
        for j in range(8):
            IFS[h * 8 + j] = a[j : j + 1, :]
            IFS[half + h * 8 + j] = b[j : j + 1, :]
            RP[h * 8 + j] = p[j : j + 1, :]
    IFR[0] = IFS[gy]

    @pl.loop(1, ny_dev)
    def _(t):
        i = py(t)
        slot = (ny_dev - t) + (i // half) * (2 * t - ny_dev)
        send(IFS.at[i], IFR.at[slot], is_sem.at[0], ir_sem.at[0], {"gy": i}).start()

    others = pl.ds(1, ny_dev - 1)
    send(IFS.at[others], IFR.at[others], is_sem.at[0], ir_sem.at[0], {"gy": py(1)}).wait()
    acc = IFR[...]
    power = RP[lax.rem(gy, half)][None]
    step = 1
    while step < ny_dev:
        acc = acc + power * jnp.concatenate([acc[ny_dev - step :], acc[: ny_dev - step]], axis=0)
        power = power * power
        step *= 2
    acc = acc * (1.0 / (1.0 - power))
    IFO[...] = jnp.concatenate([acc[ny_dev - 1 :], acc[: ny_dev - 1]], axis=0)
    IFB[gy] = IFO[0]
    sign = 1 - 2 * (gy // half)

    @pl.loop(1, ny_dev)
    def _(t):
        dev = lax.rem(gy + t * sign + ny_dev, ny_dev)
        send(IFO.at[t], IFB.at[gy], is_sem.at[1], ir_sem.at[1], {"gy": dev}).start()

    send(IFO.at[others], IFB.at[others], is_sem.at[1], ir_sem.at[1], {"gy": py(1)}).wait()
    ain = [jnp.concatenate([IFB[h * 8 + j] for j in range(8)], axis=0) for h in range(2)]
    bin_ = [jnp.concatenate([IFB[half + h * 8 + j] for j in range(8)], axis=0) for h in range(2)]

    def back(i, carry):
        y = ny - 1 - i
        at = pl.ds(pl.multiple_of(y * 8, 8), 8)
        out = []
        for h in range(2):
            b = S[h, at, :] + rate[h] * carry[h]
            SB[h, at, :] = rate[h] * carry[h]
            out.append(b)
        return tuple(out)

    lax.fori_loop(0, ny, back, tuple(bin_), unroll=8)

    def forth(y, carry):
        at = pl.ds(pl.multiple_of(y * 8, 8), 8)
        out = []
        for h in range(2):
            a = S[h, at, :] + rate[h] * carry[h]
            S[h, at, :] = scale[h] * (a + SB[h, at, :])
            out.append(a)
        return tuple(out)

    last = lax.fori_loop(0, ny, forth, tuple(ain), unroll=8)
    for h in range(2):
        S[h, ny * 8 : ny * 8 + 8, :] = scale[h] * (rate[h] * last[h] + bin_[h])
        S[h, ny * 8 + 8 : ny * 8 + 64, :] = jnp.zeros((56, 128), f32)

    def x_inverse(y0, n, put):
        for m in range(8):
            for h in range(2):
                Z[m * n : m * n + n, 128 * h : 128 * h + 128] = S[h, pl.ds(y0 * 8 + m, n, stride=8), :]
        o0 = dot3(Z[0:n, :], MATS[6], MATS[7])
        om = dot3(Z[n : 8 * n, :], MATS[4], MATS[5])
        Z[0:n, :] = o0
        Z[n : 8 * n, :] = om
        for i in range(n // 8):
            zr, zi = {}, {}
            for m in range(1, 8):
                co, si = tab_ref[m : m + 1, :], tab_ref[8 + m : 9 + m, :]
                at = m * n + 8 * i
                a, b = Z[at : at + 8, 0:128], Z[at : at + 8, 128:256]
                zr[m] = a * co - b * si
                zi[m] = a * si + b * co
            put(i, inv16(Z[8 * i : 8 * i + 8, 0:128], Z[8 * i : 8 * i + 8, 128:256], zr, zi))

    lane_8 = lanes((8, 128))

    @pl.loop(0, chunks)
    def _(c):
        y0 = pl.multiple_of(c * YC, YC)

        def put(i, x):
            edge = jnp.zeros((8, 128), f32)
            for q in range(16):
                TX2[q // 2, c, q % 2, 8 * i : 8 * i + 8, :] = x[q]
            for d in range(nx_dev):
                edge = jnp.where(lane_8 == d, roll(x[(2 * d + 2) % 16], d, 1), edge)
            EW[pl.ds(y0 + 8 * i, 8), :] = edge

        x_inverse(y0, YC, put)
        pltpu.make_async_copy(TX2.at[gx, c], RX2.at[c, gx], l2_sem.at[c]).start()
        for t in range(1, nx_dev):
            g = px(t)
            send(TX2.at[g, c], RX2.at[c, gx], s2_sem.at[c, t], r2_sem.at[c, gx], {"gx": g}).start()

    EW[ny:128, :] = jnp.zeros((128 - ny, 128), f32)
    ewt = jnp.transpose(EW[...])
    row8 = rows_of((8, 128))

    def put_north(i, x):
        for d in range(nx_dev):
            e = jnp.broadcast_to(ewt[d : d + 1, :], (8, 128))
            n0 = jnp.broadcast_to(x[2 * d][0:1], (8, 128))
            n1 = jnp.broadcast_to(x[2 * d + 1][0:1], (8, 128))
            X2[d] = jnp.where(row8 == 0, n0, jnp.where(row8 == 1, n1, e))

    x_inverse(ny, 8, put_north)
    pltpu.make_async_copy(X2.at[gx], XR.at[gx], l2_sem.at[chunks]).start()
    for t in range(1, nx_dev):
        g = px(t)
        send(X2.at[g], XR.at[gx], sx_sem.at[t], rx_sem.at[gx], {"gx": g}).start()

    @pl.loop(0, chunks)
    def _(c):
        pltpu.make_async_copy(TX2.at[gx, c], RX2.at[c, gx], l2_sem.at[c]).wait()
        for t in range(1, nx_dev):
            g = px(t)
            send(TX2.at[g, c], RX2.at[c, g], s2_sem.at[c, t], r2_sem.at[c, g], {"gx": g}).wait_recv()

    pltpu.make_async_copy(X2.at[gx], XR.at[gx], l2_sem.at[chunks]).wait()
    for t in range(1, nx_dev):
        g = px(t)
        send(X2.at[g], XR.at[g], sx_sem.at[t], rx_sem.at[g], {"gx": g}).wait_recv()

    @pl.loop(0, chunks)
    def _(c):
        for t in range(1, nx_dev):
            g = px(t)
            send(TX1.at[g, c], RX1.at[c, g], s1_sem.at[c, t], r1_sem.at[c, g], {"gx": g}).wait_send()
            send(TX2.at[g, c], RX2.at[c, g], s2_sem.at[c, t], r2_sem.at[c, g], {"gx": g}).wait_send()

    for t in range(1, nx_dev):
        g = px(t)
        send(X2.at[g], XR.at[g], sx_sem.at[t], rx_sem.at[g], {"gx": g}).wait_send()


def finish(
    U, V, WS, tn_ref, RX2, XR, TI, COEF, un_hbm, vn_hbm, wn_hbm, tn_hbm, p_hbm,
    un_ref, vn_ref, wn_ref, p_ref, EC, EX, tn_sem, out_sem,
):
    levels, ny, nx = U.shape
    chunks = ny // YC
    theta = pltpu.make_async_copy(tn_ref, tn_hbm, tn_sem.at[0])
    theta.start()
    lane_n = lanes((ny, 128))
    row8 = rows_of((8, 128))

    @pl.loop(0, chunks)
    def _(c):
        cen = pl.ds(pl.multiple_of(c * YC, YC), YC)
        for h in range(2):
            col = [RX2[c, j, h] for j in range(levels)]
            for k in range(levels):
                acc = TI[k : k + 1, :] * col[0]
                for j in range(1, levels):
                    acc = acc + TI[j * 8 + k : j * 8 + k + 1, :] * col[j]
                p_ref[k, cen, 128 * h : 128 * h + 128] = acc

    def out(i, ref, hbm, k):
        return pltpu.make_async_copy(ref.at[k], hbm.at[k], out_sem.at[i, k])

    outs = [(p_ref, p_hbm), (un_ref, un_hbm), (vn_ref, vn_hbm), (wn_ref, wn_hbm)]
    for k in range(levels):
        out(0, p_ref, p_hbm, k).start()

    east = jnp.zeros((8, 128), f32)
    for k in range(levels):
        acc = TI[k : k + 1, :] * XR[0]
        for j in range(1, levels):
            acc = acc + TI[j * 8 + k : j * 8 + k + 1, :] * XR[j]
        EX[k] = acc
        east = jnp.where(row8 == k, jnp.broadcast_to(acc[2:3, :], (8, 128)), east)
    EC[0:8, :] = east
    EC[8:128, :] = jnp.zeros((120, 128), f32)
    EC[...] = jnp.transpose(EC[...])

    for k in range(levels):
        p = p_ref[k]
        pleft, pright = p[:, :128], p[:, 128:]
        col = jnp.broadcast_to(EC[0:ny, k : k + 1], (ny, 128))
        a, b = roll(pleft, -1, 1), roll(pright, -1, 1)
        gl = jnp.where(lane_n < 127, a, b) - pleft
        gr = jnp.where(lane_n < 127, b, col) - pright
        un_ref[k] = U[k] - DT * jnp.concatenate([gl, gr], axis=1)
        out(1, un_ref, un_hbm, k).start()
        ex = EX[k]
        north = jnp.concatenate([ex[0:1, :], ex[1:2, :]], axis=1)
        shifted = roll(p, -1, 0)
        shifted = jnp.where(rows_of((ny, nx)) < ny - 1, shifted, jnp.broadcast_to(north, (ny, nx)))
        vn_ref[k] = V[k, 8 : 8 + ny, :] - DT * (shifted - p)
        out(2, vn_ref, vn_hbm, k).start()
        g = COEF[48 + k : 49 + k, :]
        if k + 1 < levels:
            wn_ref[k] = WS[k] - g * (p_ref[k + 1] - p)
        else:
            wn_ref[k] = WS[k] + g * p
        out(3, wn_ref, wn_hbm, k).start()

    theta.wait()
    for k in range(levels):
        for i, (ref, hbm) in enumerate(outs):
            out(i, ref, hbm, k).wait()


def per_device(u_face, v_face, w_face, theta_field, density, thickness):
    nx_dev = lax.axis_size("gx")
    ny_dev = lax.axis_size("gy")
    levels, ny, nx = u_face.shape
    chunks = ny // YC
    mats, tab = tables()
    vm = pltpu.VMEM
    dma = pltpu.SemaphoreType.DMA
    full = (levels, ny, nx)
    out = jax.ShapeDtypeStruct(full, f32)
    hbm = pl.BlockSpec(memory_space=pltpu.HBM)
    vmem = pl.BlockSpec(memory_space=pltpu.VMEM)
    scratch = [
        pltpu.SMEM((levels,), f32), pltpu.SMEM((levels,), f32), vm((32, 128), f32),
        vm((levels, ny + 16, nx), f32),
        vm((levels, ny + 16, nx), f32),
        vm((8, 256, 256), bf16),
        vm((64, 128), f32),
        vm((8, 8, 128), f32),
        vm((ny, 128), f32), vm((ny, 128), f32), vm((ny, 128), f32), vm((ny, 128), f32),
        vm((levels, 8, nx), f32), vm((levels, 8, nx), f32),
        vm((levels, 8, nx), f32), vm((levels, 8, nx), f32),
        vm((ny, 128), f32),
        vm((levels, 8, nx), f32),
        vm((levels, YC, nx), f32),
        vm((levels, chunks, 2, YC, 128), f32),
        vm((chunks, nx_dev, 2, YC, 128), f32),
        vm((8 * YC, 256), f32),
        vm((2, (ny + 8) * 8, 128), f32),
        vm((2, ny * 8, 128), f32),
        vm((32, 1, 128), f32), vm((32, 1, 128), f32), vm((32, 1, 128), f32), vm((32, 1, 128), f32),
        vm((16, 1, 128), f32),
        vm((nx_dev, chunks, 2, YC, 128), f32),
        vm((nx_dev, 8, 128), f32),
        vm((128, 128), f32),
        dma((8,)), dma((4,)), dma((4,)),
        dma((chunks, nx_dev)), dma((chunks, nx_dev)), dma((chunks,)),
        dma((2,)), dma((2,)),
        dma((chunks, nx_dev)), dma((chunks, nx_dev)), dma((chunks + 1,)),
        dma((nx_dev,)), dma((nx_dev,)),
    ]
    mid = pl.pallas_call(
        functools.partial(kernel, nx_dev, ny_dev),
        out_shape=(
            out,
            jax.ShapeDtypeStruct((levels, ny + 8, nx), f32),
            out,
            out,
            jax.ShapeDtypeStruct((chunks, levels, 2, YC, 128), f32),
            jax.ShapeDtypeStruct((levels, 8, 128), f32),
            jax.ShapeDtypeStruct((64, 128), f32),
            jax.ShapeDtypeStruct((56, 256), f32),
        ),
        in_specs=[hbm] * 8,
        out_specs=(vmem,) * 8,
        scratch_shapes=scratch,
        compiler_params=pltpu.CompilerParams(
            collective_id=0, has_side_effects=True, vmem_limit_bytes=36 << 20
        ),
        name="substep",
    )(*(
        pltpu.with_memory_space_constraint(a, pltpu.HBM)
        for a in (density, thickness, jnp.asarray(tab), u_face, v_face, w_face, theta_field, jnp.asarray(mats))
    ))
    return pl.pallas_call(
        finish,
        out_shape=(out,) * 5,
        in_specs=[vmem] * 8,
        out_specs=(hbm,) * 5,
        scratch_shapes=[
            vm(full, f32), vm(full, f32), vm(full, f32), vm(full, f32),
            vm((128, 128), f32), vm((levels, 8, 128), f32), dma((1,)), dma((4, levels)),
        ],
        compiler_params=pltpu.CompilerParams(vmem_limit_bytes=24 << 20),
        name="finish",
    )(*mid)


def solution(mesh):
    spec = P(None, "gy", "gx")
    return jax.shard_map(
        per_device,
        mesh=mesh,
        in_specs=(spec, spec, spec, spec, P(), P()),
        out_specs=(spec,) * 5,
        check_vma=False,
    )
```

```python
import functools

import jax
import jax.numpy as jnp
import numpy as np
from jax import lax
from jax.experimental import pallas as pl
from jax.experimental.pallas import tpu as pltpu
from jax.sharding import PartitionSpec as P

DT = 0.2
f32 = jnp.float32
bf16 = jnp.bfloat16
MESH = pl.DeviceIdType.MESH
C1, C2, C3 = float(np.cos(np.pi / 8)), float(np.cos(np.pi / 4)), float(np.cos(3 * np.pi / 8))
YC = 16


def split_bf16(a):
    hi = a.astype(jnp.bfloat16)
    lo = (a - hi.astype(np.float64)).astype(jnp.bfloat16)
    return hi, lo


@functools.cache
def tables():
    n_x = 2048
    l = np.arange(128)
    n = np.arange(128)

    def cas(t):
        return np.cos(t) + np.sin(t)

    cos = np.cos(2 * np.pi * np.outer(l, n) / 128)
    sin = np.sin(2 * np.pi * np.outer(l, n) / 128)
    zero = np.zeros((128, 128))
    fw = np.block([[cos, -sin], [sin, cos]])
    b0 = cas(2 * np.pi * np.outer(l, n) / 128)
    b8 = cas(2 * np.pi * np.outer(l, 16 * n + 8) / n_x)
    fb = np.block([[b0, zero], [zero, b8]])
    mats = []
    for m in (fw, fb, fw.T * (2 / n_x), fb.T * (1 / n_x)):
        mats.extend(split_bf16(m))
    mats = np.stack(mats)
    tw = np.arange(8)[:, None] * l[None, :] * (2 * np.pi / n_x)
    k_lo = 16 * n[None, :] + np.arange(8)[:, None]
    k_hi = k_lo.copy()
    k_hi[0] += 8
    tab = np.concatenate(
        [np.cos(tw), np.sin(tw), 4 * np.sin(np.pi * k_lo / n_x) ** 2, 4 * np.sin(np.pi * k_hi / n_x) ** 2]
    ).astype(np.float32)
    return mats, tab


def fwd16(x):
    s = [x[q] + x[q + 8] for q in range(8)]
    d = [x[q] - x[q + 8] for q in range(8)]
    t = [s[q] + s[q + 4] for q in range(4)]
    e = [s[q] - s[q + 4] for q in range(4)]
    t02, t13 = t[0] + t[2], t[1] + t[3]
    re, im = {}, {}
    y0, y8 = t02 + t13, t02 - t13
    re[4], im[4] = t[0] - t[2], t[3] - t[1]
    a, b = C2 * (e[1] - e[3]), C2 * (e[1] + e[3])
    re[2], re[6] = e[0] + a, e[0] - a
    im[2], im[6] = -(e[2] + b), e[2] - b
    u = [None] + [d[q] - d[8 - q] for q in (1, 2, 3)]
    v = [None] + [d[q] + d[8 - q] for q in (1, 2, 3)]
    g = C2 * u[2]
    g1, g2 = d[0] + g, d[0] - g
    h1, h2 = C1 * u[1] + C3 * u[3], C3 * u[1] - C1 * u[3]
    re[1], re[7], re[3], re[5] = g1 + h1, g1 - h1, g2 + h2, g2 - h2
    k = C2 * v[2]
    k1, k2 = k + d[4], k - d[4]
    m1, m2 = C3 * v[1] + C1 * v[3], C1 * v[1] - C3 * v[3]
    im[1], im[7], im[3], im[5] = -(m1 + k1), k1 - m1, -(m2 + k2), k2 - m2
    return y0, y8, re, im


def inv16(a0, a8, zr, zi):
    p1, m1, p3, m3 = zr[1] + zr[7], zr[1] - zr[7], zr[3] + zr[5], zr[3] - zr[5]
    r1, s1, r3, s3 = zi[1] + zi[7], zi[1] - zi[7], zi[3] + zi[5], zi[3] - zi[5]
    o = [None] * 8
    o[0] = p1 + p3
    o[4] = s3 - s1
    cs = [None, C1 * m1 + C3 * m3, C2 * (p1 - p3), C3 * m1 - C1 * m3]
    sn = [None, C3 * r1 + C1 * r3, C2 * (s1 + s3), C1 * r1 - C3 * r3]
    for q in (1, 2, 3):
        o[q] = cs[q] - sn[q]
        o[8 - q] = -cs[q] - sn[q]
    ap, am = a0 + a8, a0 - a8
    g = [ap + zr[4], am - zi[4], ap - zr[4], am + zi[4]]
    w1, w2 = C2 * (zr[2] - zr[6]), C2 * (zi[2] + zi[6])
    h = [zr[2] + zr[6], w1 - w2, zi[6] - zi[2], -w1 - w2]
    ev = [g[q] + h[q] for q in range(4)] + [g[q] - h[q] for q in range(4)]
    return [ev[q] + o[q] for q in range(8)] + [ev[q] - o[q] for q in range(8)]


def dot3(x, hi, lo):
    xh = x.astype(bf16)
    xl = (x - xh.astype(f32)).astype(bf16)
    out = jnp.dot(xh, hi, preferred_element_type=f32)
    out += jnp.dot(xl, hi, preferred_element_type=f32)
    out += jnp.dot(xh, lo, preferred_element_type=f32)
    return out


def flux(qm2, qm1, q0, q1, q2, q3, c):
    s = 37.0 * (q0 + q1) - 8.0 * (qm1 + q2) + (qm2 + q3)
    d = 10.0 * (q1 - q0) - 5.0 * (q2 - qm1) + (q3 - qm2)
    return c * s - jnp.abs(c) * d


def roll(x, shift, axis):
    n = x.shape[axis]
    shift = shift % n
    return x if shift == 0 else pltpu.roll(x, shift, axis)


def lanes(shape):
    return lax.broadcasted_iota(jnp.int32, shape, len(shape) - 1)


def rows_of(shape):
    return lax.broadcasted_iota(jnp.int32, shape, 0)


def kernel(
    nx_dev, ny_dev,
    den_hbm, thk_hbm, tab_hbm, u_hbm, v_hbm, w_hbm, th_hbm, mats_hbm,
    U, V, WS, tn_ref, p_ref, XR, TI, COEF,
    den_ref, thk_ref, tab_ref, W, TH, MATS, TF, LAM,
    PE_S, PW_S, PE_R, PW_R, YN_S, YS_S, YN_R, YS_R, FPK, FYP,
    SRC, TX1, RX1, Z, S, SA, SB, PWR, IFS, IFR, CBS, CBR, INS, INR, TX2, RX2, X2, EW,
    in_sem, hs_sem, hr_sem, s1_sem, r1_sem, l1_sem, is_sem, ir_sem, s2_sem, r2_sem, l2_sem,
    sx_sem, rx_sem, near_sem,
):
    gx = lax.axis_index("gx")
    gy = lax.axis_index("gy")
    levels, ny, nx = u_hbm.shape
    chunks = ny // YC

    def px(t):
        return lax.rem(gx + t, nx_dev)

    def py(t):
        return lax.rem(gy + t, ny_dev)

    n_chips = ny_dev // 2
    chip, core = gy // 2, lax.rem(gy, 2)

    def chip_at(t):
        return 2 * lax.rem(chip + t, n_chips) + core

    def greet(stage):
        for t in (2**stage, n_chips - 2**stage):
            pl.semaphore_signal(near_sem.at[stage], inc=1, device_id={"gy": chip_at(t)}, device_id_type=MESH)

    def greeted(stage):
        pl.semaphore_wait(near_sem.at[stage], 2)

    mid = pl.ds(8, ny)
    small = [
        pltpu.make_async_copy(den_hbm, den_ref, in_sem.at[5]),
        pltpu.make_async_copy(thk_hbm, thk_ref, in_sem.at[6]),
        pltpu.make_async_copy(tab_hbm, tab_ref, in_sem.at[7]),
    ]
    loads = [
        pltpu.make_async_copy(w_hbm, W.at[:, mid, :], in_sem.at[0]),
        pltpu.make_async_copy(th_hbm, TH.at[:, mid, :], in_sem.at[1]),
        pltpu.make_async_copy(u_hbm, U, in_sem.at[2]),
        pltpu.make_async_copy(v_hbm, V.at[:, mid, :], in_sem.at[3]),
        pltpu.make_async_copy(mats_hbm, MATS, in_sem.at[4]),
    ]
    for cp in small + loads:
        cp.start()

    barrier = pltpu.get_barrier_semaphore()
    for t in range(1, nx_dev):
        pl.semaphore_signal(barrier, inc=1, device_id={"gx": px(t)}, device_id_type=MESH)

    for t in (1, ny_dev - 1):
        pl.semaphore_signal(barrier, inc=1, device_id={"gy": py(t)}, device_id_type=MESH)
    for t in (1, n_chips - 1):
        pl.semaphore_signal(barrier, inc=1, device_id={"gy": chip_at(t)}, device_id_type=MESH)

    for cp in loads[:4]:
        cp.wait()
    lane_c = lanes((YC, 128))

    @pl.loop(0, chunks)
    def _(c):
        y0 = pl.multiple_of(c * YC, YC)
        east = jnp.zeros((YC, 128), f32)
        west = jnp.zeros((YC, 128), f32)
        for k in range(levels):
            o = 16 * k
            rows = pl.ds(y0 + 8, YC)
            wl, wr = W[k, rows, 0:128], W[k, rows, 128:256]
            tl, tr = TH[k, rows, 0:128], TH[k, rows, 128:256]
            ur = U[k, pl.ds(y0, YC), 128:256]
            east = jnp.where((lane_c >= o) & (lane_c < o + 3), roll(wr, o - 125, 1), east)
            east = jnp.where((lane_c >= o + 3) & (lane_c < o + 6), roll(tr, o + 3 - 125, 1), east)
            east = jnp.where(lane_c == o + 6, roll(ur, o + 6 - 127, 1), east)
            west = jnp.where((lane_c >= o) & (lane_c < o + 3), roll(wl, o, 1), west)
            west = jnp.where((lane_c >= o + 3) & (lane_c < o + 6), roll(tl, o + 3, 1), west)
        PE_S[pl.ds(y0, YC), :] = east
        PW_S[pl.ds(y0, YC), :] = west

    for k in range(levels):
        a, b, c = W[k, ny : ny + 8, :], TH[k, ny : ny + 8, :], V[k, ny : ny + 8, :]
        row = rows_of((8, nx))
        YN_S[k] = jnp.where(row < 3, roll(a, 3, 0), jnp.where(row < 6, roll(b, 6, 0), roll(c, 7, 0)))
        a, b = W[k, 8:16, :], TH[k, 8:16, :]
        YS_S[k] = jnp.where(row < 3, a, roll(b, 3, 0))

    pl.semaphore_wait(barrier, nx_dev - 1 + 4)
    halos = []
    for i, (src, dst, where) in enumerate(
        [
            (PE_S, PE_R, {"gx": px(1)}),
            (PW_S, PW_R, {"gx": px(nx_dev - 1)}),
            (YN_S, YN_R, {"gy": py(1)}),
            (YS_S, YS_R, {"gy": py(ny_dev - 1)}),
        ]
    ):
        cp = pltpu.make_async_remote_copy(
            src_ref=src, dst_ref=dst, send_sem=hs_sem.at[i], recv_sem=hr_sem.at[i],
            device_id=where, device_id_type=MESH,
        )
        cp.start()
        halos.append(cp)

    for cp in small:
        cp.wait()

    r8 = rows_of((8, 128))
    j8 = lax.rem(lanes((8, 128)), 8)
    den = jnp.zeros((8, 128), f32)
    thk = jnp.zeros((8, 128), f32)
    for k in range(levels):
        den = jnp.where(r8 == k, den_ref[k], den)
        thk = jnp.where(r8 == k, thk_ref[k], thk)

    def lift(a):
        return jnp.where(r8 == 7, a, roll(a, -1, 0))

    def below(a):
        return jnp.where(r8 == 0, 0.0, roll(a, 1, 0))

    lden = lift(den)
    fd = (den + lden) / 2.0
    fs = (thk + lift(thk)) / 2.0
    mass = den * thk
    zw = (DT / 60.0) / (fd * fs)
    zt = (DT / 60.0) / mass
    sc = (1.0 / DT) / mass
    coefs = [lden * zw, below(lden) * zw, fd * zt, below(fd) * zt, fd * sc, below(fd) * sc, DT / fs]
    for i, a in enumerate(coefs):
        COEF[i * 8 : i * 8 + 8, :] = jnp.concatenate([a, a], axis=1)

    cond = fd / fs
    diag = jnp.sqrt(cond / mass)
    off = -jnp.sqrt(cond / lift(mass))
    b_mat = jnp.where(j8 == r8, diag, jnp.where(j8 == r8 + 1, off, 0.0))
    q_mat = jnp.where(j8 == r8, 1.0, 0.0)
    pairs = [
        (4, j8 < 4),
        (1, lax.rem(j8, 2) == 0), (1, lax.rem(j8, 2) == 1),
        (3, lax.rem(j8, 2) == 0), (3, lax.rem(j8, 2) == 1),
        (2, lax.rem(j8, 4) < 2), (2, lax.rem(j8, 4) >= 2),
    ]

    def total(x):
        return ((x[0] + x[1]) + (x[2] + x[3])) + ((x[4] + x[5]) + (x[6] + x[7]))

    def partner(x, o, ahead):
        if o == 4:
            return roll(x, 4, 1)
        return jnp.where(ahead, roll(x, -o, 1), roll(x, o, 1))

    def sweep(_, carry):
        b, q = list(carry[:8]), list(carry[8:])
        for o, ahead in pairs:
            bp = [partner(x, o, ahead) for x in b]
            al = total([x * x for x in b])
            ap = total([x * x for x in bp])
            g = total([x * y for x, y in zip(b, bp)])
            d = ap - al
            h2 = d * d + 4.0 * g * g
            ok = h2 > 1e-30
            rh = lax.rsqrt(jnp.where(ok, h2, 1.0))
            c2 = 0.5 + 0.5 * jnp.abs(d) * rh
            rc = lax.rsqrt(c2)
            sg = jnp.where(d > 0.0, g, jnp.where(d < 0.0, -g, jnp.where(ahead, g, -g)))
            c = jnp.where(ok, c2 * rc, 1.0)
            s = jnp.where(ok, sg * rh * rc, 0.0)
            qp = [partner(x, o, ahead) for x in q]
            b = [c * x - s * y for x, y in zip(b, bp)]
            q = [c * x - s * y for x, y in zip(q, qp)]
        return (*b, *q)

    start = [jnp.broadcast_to(m[k : k + 1], (8, 128)) for m in (b_mat, q_mat) for k in range(8)]
    got = lax.fori_loop(0, 5, sweep, tuple(start))
    norm = 1.0 / total([x * x for x in got[8:]])
    lam = total([x * x for x in got[:8]]) * norm
    unit = jnp.sqrt(norm)
    q_mat = jnp.zeros((8, 128), f32)
    for k in range(8):
        q_mat = jnp.where(r8 == k, got[8 + k] * unit, q_mat)
    root = jnp.sqrt(mass)
    qf = q_mat * root
    qi = q_mat / root
    for j in range(8):
        TF[j * 8 : j * 8 + 8, :] = jnp.broadcast_to(qf[:, j : j + 1], (8, 128))
        TI[j * 8 : j * 8 + 8, :] = jnp.broadcast_to(qi[:, j : j + 1], (8, 128))
        LAM[j] = jnp.broadcast_to(lam[:, j : j + 1], (8, 128))

    greet(0)
    for cp in halos:
        cp.wait()
    greeted(0)
    greet(1)

    for k in range(levels):
        n8, s8 = YN_R[k], YS_R[k]
        W[k, 0:8, :] = roll(n8, 5, 0)
        TH[k, 0:8, :] = roll(n8, 2, 0)
        V[k, 0:8, :] = roll(n8, 1, 0)
        W[k, ny + 8 : ny + 16, :] = s8
        TH[k, ny + 8 : ny + 16, :] = roll(s8, 5, 0)

    lane_n = lanes((ny, 128))
    ph, po = PE_R[...], PW_S[...]
    lane_m = lax.rem(lane_n, 16)
    u_th = roll(ph, -3, 1)
    u_top = jnp.where(lane_n >= 112, roll(ph, -6, 1), roll(ph, -22, 1))
    u_w = (roll(ph, -6, 1) + u_top) / 2.0
    FPK[...] = flux(
        ph, roll(ph, -1, 1), roll(ph, -2, 1), po, roll(po, -1, 1), roll(po, -2, 1),
        jnp.where(lane_m == 0, u_w, u_th),
    )

    def nxt(k):
        return min(k + 1, levels - 1)

    def y_shifts(block, n):
        return [roll(block, -s, 0)[8 : 8 + n] if s else block[8 : 8 + n] for s in range(-2, 4)]

    def south_flux(field, first, lifted):
        for k in range(levels):
            block = field[k, 0:16, :]
            qs = [roll(block, -s, 0)[0:8] for s in range(-2, 4)]
            c = V[k, 0:8, :]
            if lifted:
                c = (c + V[nxt(k), 0:8, :]) / 2.0
            FYP[k] = flux(*qs, c)

    def advect(field, k, y0, extra, lifted, fz_below, zi):
        o = 16 * k + extra
        rows = pl.ds(y0 + 8, YC)
        cen = pl.ds(y0, YC)
        block = field[k, pl.ds(y0, YC + 16), :]
        q = block[8 : 8 + YC]
        left, right = q[:, :128], q[:, 128:]
        pe, pw = PW_R[cen, :], PE_R[cen, :]
        ls, rs = [], []
        for s in range(-2, 4):
            if s == 0:
                ls.append(left)
                rs.append(right)
                continue
            a, b = roll(left, -s, 1), roll(right, -s, 1)
            if s > 0:
                ls.append(jnp.where(lane_c < 128 - s, a, b))
                rs.append(jnp.where(lane_c < 128 - s, b, roll(pe, -s - o, 1)))
            else:
                ls.append(jnp.where(lane_c >= -s, a, roll(pw, -s - 3 - o, 1)))
                rs.append(jnp.where(lane_c >= -s, b, a))
        u, v, w = U[k, cen, :], V[k, rows, :], W[k, rows, :]
        if lifted:
            u = (u + U[nxt(k), cen, :]) / 2.0
            v = (v + V[nxt(k), rows, :]) / 2.0
            w = (w + W[nxt(k), rows, :]) / 2.0
        fl = flux(*ls, u[:, :128])
        fr = flux(*rs, u[:, 128:])
        fl_roll = roll(fl, 1, 1)
        wl = jnp.where(lane_c >= 1, fl_roll, roll(FPK[cen, :], -o, 1))
        wr = jnp.where(lane_c >= 1, roll(fr, 1, 1), fl_roll)
        div = jnp.concatenate([fl - wl, fr - wr], axis=1)
        fy = flux(*y_shifts(block, YC), v)
        prev = roll(jnp.concatenate([FYP[k], fy], axis=0), 1, 0)[8:]
        FYP[k] = fy[YC - 8 :]
        div = div + (fy - prev)
        zq = [field[min(max(k + s, 0), levels - 1), rows, :] for s in range(-2, 4)]
        fz = flux(*zq, w)
        tend = (-DT / 60.0) * div - COEF[zi + k : zi + k + 1, :] * fz
        if k > 0:
            tend = tend + COEF[zi + 8 + k : zi + 9 + k, :] * fz_below
        return q, tend, fz

    def send(src, dst, s_sem, r_sem, who):
        return pltpu.make_async_remote_copy(
            src_ref=src, dst_ref=dst, send_sem=s_sem, recv_sem=r_sem,
            device_id=who, device_id_type=MESH,
        )

    south_flux(W, 0, True)

    @pl.loop(0, chunks)
    def _(c):
        y0 = pl.multiple_of(c * YC, YC)
        rows = pl.ds(y0 + 8, YC)
        cen = pl.ds(y0, YC)
        fz, star_below = None, None
        for k in range(levels):
            q, tend, fz = advect(W, k, y0, 0, True, fz, 0)
            star = q + tend + (0.5 * DT) * (TH[k, rows, :] + TH[nxt(k), rows, :])
            WS[k, cen, :] = star
            u = U[k, cen, :]
            ul = roll(u[:, :128], 1, 1)
            uw = jnp.where(lane_c >= 1, ul, roll(PE_R[cen, :], -(16 * k + 6), 1))
            ue = jnp.where(lane_c >= 1, roll(u[:, 128:], 1, 1), ul)
            vb = V[k, pl.ds(y0, YC + 8), :]
            dv = (vb - roll(vb, 1, 0))[8:]
            src = (u - jnp.concatenate([uw, ue], axis=1) + dv) * (1.0 / DT)
            src = src + COEF[32 + k : 33 + k, :] * star
            if k > 0:
                src = src - COEF[40 + k : 41 + k, :] * star_below
            star_below = star
            SRC[k] = src
        for h in range(2):
            hs = slice(128 * h, 128 * h + 128)
            col = [SRC[k, :, hs] for k in range(levels)]
            for j in range(levels):
                acc = TF[j * 8 : j * 8 + 1, :] * col[0]
                for k in range(1, levels):
                    acc = acc + TF[j * 8 + k : j * 8 + k + 1, :] * col[k]
                TX1[j, c, h] = acc
        pltpu.make_async_copy(TX1.at[gx, c], RX1.at[c, gx], l1_sem.at[c]).start()
        for t in range(1, nx_dev):
            g = px(t)
            send(TX1.at[g, c], RX1.at[c, gx], s1_sem.at[c, t], r1_sem.at[c, gx], {"gx": g}).start()

    south_flux(TH, 0, False)

    @pl.loop(0, chunks)
    def _(c):
        y0 = pl.multiple_of(c * YC, YC)
        fz = None
        for k in range(levels):
            q, tend, fz = advect(TH, k, y0, 3, False, fz, 16)
            tn_ref[k, pl.ds(y0, YC), :] = q + tend

    greeted(1)
    greet(2)

    lam_g = LAM[gx]
    rate, scale = [], []
    for h in range(2):
        mu = lam_g + tab_ref[16 + 8 * h : 24 + 8 * h, :]
        rt = jnp.sqrt(mu * mu + 4.0 * mu)
        rate.append(2.0 / (2.0 + mu + rt))
        scale.append(-1.0 / rt)

    loads[4].wait()

    def x_forward(c, carry):
        y0 = pl.multiple_of(c * YC, YC)
        pltpu.make_async_copy(TX1.at[gx, c], RX1.at[c, gx], l1_sem.at[c]).wait()
        for t in range(1, nx_dev):
            g = px(t)
            send(TX1.at[g, c], RX1.at[c, g], s1_sem.at[c, t], r1_sem.at[c, g], {"gx": g}).wait_recv()
        for i in range(YC // 8):
            sub = slice(8 * i, 8 * i + 8)
            x = [RX1[c, q // 2, q % 2, sub, :] for q in range(16)]
            y_0, y_8, re, im = fwd16(x)
            Z[8 * i : 8 * i + 8, 0:128] = y_0
            Z[8 * i : 8 * i + 8, 128:256] = y_8
            for m in range(1, 8):
                co, si = tab_ref[m : m + 1, :], tab_ref[8 + m : 9 + m, :]
                at = m * YC + 8 * i
                Z[at : at + 8, 0:128] = re[m] * co + im[m] * si
                Z[at : at + 8, 128:256] = im[m] * co - re[m] * si
        o0 = dot3(Z[0:YC, :], MATS[2], MATS[3])
        om = dot3(Z[YC : 8 * YC, :], MATS[0], MATS[1])
        for m in range(8):
            val = o0 if m == 0 else om[(m - 1) * YC : m * YC]
            for h in range(2):
                S[h, pl.ds(y0 * 8 + m, YC, stride=8), :] = val[:, 128 * h : 128 * h + 128]
        a0, a1, b0, b1, p0, p1 = carry
        for i in range(YC):
            at = pl.ds(y0 * 8 + 8 * i, 8)
            f0, f1 = S[0, at, :], S[1, at, :]
            a0, a1 = f0 + rate[0] * a0, f1 + rate[1] * a1
            b0, b1 = b0 + p0 * f0, b1 + p1 * f1
            SA[0, at, :], SA[1, at, :] = a0, a1
            PWR[0, at, :], PWR[1, at, :] = p0, p1
            p0, p1 = p0 * rate[0], p1 * rate[1]
        return a0, a1, b0, b1, p0, p1

    zero = jnp.zeros((8, 128), f32)
    one = jnp.ones((8, 128), f32)
    a0, a1, b0, b1, p0, p1 = lax.fori_loop(0, chunks, x_forward, (zero, zero, zero, zero, one, one))

    greeted(2)

    first = core == 0
    whole = [p0, p1]
    mine = []
    for h, (a, b) in enumerate([(a0, b0), (a1, b1)]):
        IFS[h] = jnp.where(first, a, b)
        mine.append(jnp.where(first, b, a))
    pair = {"gy": gy + 1 - 2 * core}
    swap = send(IFS, IFR, is_sem.at[0], ir_sem.at[0], pair)
    swap.start()
    swap.wait()
    for h in range(2):
        CBS[h] = mine[h] + whole[h] * IFR[h]
    sign = 2 * core - 1
    for t in (4, 12, 11, 5, 3, 13, 10, 6, 2, 14, 8, 9, 7, 1, 15):
        dev = 2 * lax.rem(chip + t * sign + n_chips, n_chips) + core
        send(CBS, CBR.at[t], is_sem.at[1], ir_sem.at[1], {"gy": dev}).start()

    def back(i, carry):
        y = ny - 1 - i
        at = pl.ds(pl.multiple_of(y * 8, 8), 8)
        out = []
        for h in range(2):
            b = rate[h] * carry[h]
            SB[h, at, :] = SA[h, at, :] + b
            out.append(S[h, at, :] + b)
        return tuple(out)

    lax.fori_loop(0, ny, back, (zero, zero), unroll=8)

    others = pl.ds(1, n_chips - 1)
    send(CBR.at[others], CBR.at[others], is_sem.at[1], ir_sem.at[1], pair).wait()
    into = []
    for h in range(2):
        ratio = whole[h] * whole[h]
        acc = CBS[h]
        for t in range(n_chips - 1, 0, -1):
            acc = CBR[t, h] + ratio * acc
        full = ratio
        n = 1
        while n < n_chips:
            full = full * full
            n *= 2
        into.append(acc / (1.0 - full))
        INS[h] = into[h]
    swap = send(INS, INR, is_sem.at[2], ir_sem.at[2], pair)
    swap.start()
    swap.wait()
    ain, bin_ = [], []
    for h in range(2):
        own = IFR[h] + whole[h] * into[h]
        ain.append(jnp.where(first, INR[h], own))
        bin_.append(jnp.where(first, own, INR[h]))
    ra = [rate[h] * ain[h] for h in range(2)]
    rb = [rate[h] * bin_[h] for h in range(2)]

    def correct(y0, n):
        for i in range(n):
            at = pl.ds(y0 * 8 + 8 * i, 8)
            mirror = pl.ds((ny - 1 - i) * 8 - y0 * 8, 8)
            for h in range(2):
                S[h, at, :] = scale[h] * (SB[h, at, :] + PWR[h, at, :] * ra[h] + PWR[h, mirror, :] * rb[h])

    end = slice((ny - 1) * 8, ny * 8)
    for h in range(2):
        last = SA[h, end, :] + PWR[h, end, :] * ra[h]
        S[h, ny * 8 : ny * 8 + 8, :] = scale[h] * (rate[h] * last + bin_[h])
        S[h, ny * 8 + 8 : ny * 8 + 64, :] = jnp.zeros((56, 128), f32)

    def x_inverse(y0, n, put):
        for m in range(8):
            for h in range(2):
                Z[m * n : m * n + n, 128 * h : 128 * h + 128] = S[h, pl.ds(y0 * 8 + m, n, stride=8), :]
        o0 = dot3(Z[0:n, :], MATS[6], MATS[7])
        om = dot3(Z[n : 8 * n, :], MATS[4], MATS[5])
        Z[0:n, :] = o0
        Z[n : 8 * n, :] = om
        for i in range(n // 8):
            zr, zi = {}, {}
            for m in range(1, 8):
                co, si = tab_ref[m : m + 1, :], tab_ref[8 + m : 9 + m, :]
                at = m * n + 8 * i
                a, b = Z[at : at + 8, 0:128], Z[at : at + 8, 128:256]
                zr[m] = a * co - b * si
                zi[m] = a * si + b * co
            put(i, inv16(Z[8 * i : 8 * i + 8, 0:128], Z[8 * i : 8 * i + 8, 128:256], zr, zi))

    lane_8 = lanes((8, 128))

    @pl.loop(0, chunks)
    def _(c):
        y0 = pl.multiple_of(c * YC, YC)

        def put(i, x):
            edge = jnp.zeros((8, 128), f32)
            for q in range(16):
                TX2[q // 2, c, q % 2, 8 * i : 8 * i + 8, :] = x[q]
            for d in range(nx_dev):
                edge = jnp.where(lane_8 == d, roll(x[(2 * d + 2) % 16], d, 1), edge)
            EW[pl.ds(y0 + 8 * i, 8), :] = edge

        correct(y0, YC)
        x_inverse(y0, YC, put)
        pltpu.make_async_copy(TX2.at[gx, c], RX2.at[c, gx], l2_sem.at[c]).start()
        for t in range(1, nx_dev):
            g = px(t)
            send(TX2.at[g, c], RX2.at[c, gx], s2_sem.at[c, t], r2_sem.at[c, gx], {"gx": g}).start()

    EW[ny:128, :] = jnp.zeros((128 - ny, 128), f32)
    ewt = jnp.transpose(EW[...])
    row8 = rows_of((8, 128))

    def put_north(i, x):
        for d in range(nx_dev):
            e = jnp.broadcast_to(ewt[d : d + 1, :], (8, 128))
            n0 = jnp.broadcast_to(x[2 * d][0:1], (8, 128))
            n1 = jnp.broadcast_to(x[2 * d + 1][0:1], (8, 128))
            X2[d] = jnp.where(row8 == 0, n0, jnp.where(row8 == 1, n1, e))

    x_inverse(ny, 8, put_north)
    pltpu.make_async_copy(X2.at[gx], XR.at[gx], l2_sem.at[chunks]).start()
    for t in range(1, nx_dev):
        g = px(t)
        send(X2.at[g], XR.at[gx], sx_sem.at[t], rx_sem.at[gx], {"gx": g}).start()

    @pl.loop(0, chunks)
    def _(c):
        pltpu.make_async_copy(TX2.at[gx, c], RX2.at[c, gx], l2_sem.at[c]).wait()
        for t in range(1, nx_dev):
            g = px(t)
            send(TX2.at[g, c], RX2.at[c, g], s2_sem.at[c, t], r2_sem.at[c, g], {"gx": g}).wait_recv()
        cen = pl.ds(pl.multiple_of(c * YC, YC), YC)
        for h in range(2):
            col = [RX2[c, j, h] for j in range(levels)]
            for k in range(levels):
                acc = TI[k : k + 1, :] * col[0]
                for j in range(1, levels):
                    acc = acc + TI[j * 8 + k : j * 8 + k + 1, :] * col[j]
                p_ref[k, cen, 128 * h : 128 * h + 128] = acc

    pltpu.make_async_copy(X2.at[gx], XR.at[gx], l2_sem.at[chunks]).wait()
    for t in range(1, nx_dev):
        g = px(t)
        send(X2.at[g], XR.at[g], sx_sem.at[t], rx_sem.at[g], {"gx": g}).wait_recv()

    @pl.loop(0, chunks)
    def _(c):
        for t in range(1, nx_dev):
            g = px(t)
            send(TX1.at[g, c], RX1.at[c, g], s1_sem.at[c, t], r1_sem.at[c, g], {"gx": g}).wait_send()
            send(TX2.at[g, c], RX2.at[c, g], s2_sem.at[c, t], r2_sem.at[c, g], {"gx": g}).wait_send()

    for t in range(1, nx_dev):
        g = px(t)
        send(X2.at[g], XR.at[g], sx_sem.at[t], rx_sem.at[g], {"gx": g}).wait_send()


def finish(
    U, V, WS, tn_ref, p_ref, XR, TI, COEF, un_hbm, vn_hbm, wn_hbm, tn_hbm, p_hbm,
    un_ref, vn_ref, wn_ref, EC, EX, tn_sem, out_sem,
):
    levels, ny, nx = U.shape
    theta = pltpu.make_async_copy(tn_ref, tn_hbm, tn_sem.at[0])
    theta.start()
    lane_n = lanes((ny, 128))
    row8 = rows_of((8, 128))

    def out(i, ref, hbm, k):
        return pltpu.make_async_copy(ref.at[k], hbm.at[k], out_sem.at[i, k])

    outs = [(p_ref, p_hbm), (un_ref, un_hbm), (vn_ref, vn_hbm), (wn_ref, wn_hbm)]
    for k in range(levels):
        out(0, p_ref, p_hbm, k).start()

    east = jnp.zeros((8, 128), f32)
    for k in range(levels):
        acc = TI[k : k + 1, :] * XR[0]
        for j in range(1, levels):
            acc = acc + TI[j * 8 + k : j * 8 + k + 1, :] * XR[j]
        EX[k] = acc
        east = jnp.where(row8 == k, jnp.broadcast_to(acc[2:3, :], (8, 128)), east)
    EC[0:8, :] = east
    EC[8:128, :] = jnp.zeros((120, 128), f32)
    EC[...] = jnp.transpose(EC[...])

    for k in range(levels):
        p = p_ref[k]
        pleft, pright = p[:, :128], p[:, 128:]
        col = jnp.broadcast_to(EC[0:ny, k : k + 1], (ny, 128))
        a, b = roll(pleft, -1, 1), roll(pright, -1, 1)
        gl = jnp.where(lane_n < 127, a, b) - pleft
        gr = jnp.where(lane_n < 127, b, col) - pright
        un_ref[k] = U[k] - DT * jnp.concatenate([gl, gr], axis=1)
        out(1, un_ref, un_hbm, k).start()
        ex = EX[k]
        north = jnp.concatenate([ex[0:1, :], ex[1:2, :]], axis=1)
        shifted = roll(p, -1, 0)
        shifted = jnp.where(rows_of((ny, nx)) < ny - 1, shifted, jnp.broadcast_to(north, (ny, nx)))
        vn_ref[k] = V[k, 8 : 8 + ny, :] - DT * (shifted - p)
        out(2, vn_ref, vn_hbm, k).start()
        g = COEF[48 + k : 49 + k, :]
        if k + 1 < levels:
            wn_ref[k] = WS[k] - g * (p_ref[k + 1] - p)
        else:
            wn_ref[k] = WS[k] + g * p
        out(3, wn_ref, wn_hbm, k).start()

    theta.wait()
    for k in range(levels):
        for i, (ref, hbm) in enumerate(outs):
            out(i, ref, hbm, k).wait()


def per_device(u_face, v_face, w_face, theta_field, density, thickness):
    nx_dev = lax.axis_size("gx")
    ny_dev = lax.axis_size("gy")
    levels, ny, nx = u_face.shape
    chunks = ny // YC
    mats, tab = tables()
    vm = pltpu.VMEM
    dma = pltpu.SemaphoreType.DMA
    full = (levels, ny, nx)
    out = jax.ShapeDtypeStruct(full, f32)
    hbm = pl.BlockSpec(memory_space=pltpu.HBM)
    vmem = pl.BlockSpec(memory_space=pltpu.VMEM)
    scratch = [
        pltpu.SMEM((levels,), f32), pltpu.SMEM((levels,), f32), vm((32, 128), f32),
        vm((levels, ny + 16, nx), f32),
        vm((levels, ny + 16, nx), f32),
        vm((8, 256, 256), bf16),
        vm((64, 128), f32),
        vm((8, 8, 128), f32),
        vm((ny, 128), f32), vm((ny, 128), f32), vm((ny, 128), f32), vm((ny, 128), f32),
        vm((levels, 8, nx), f32), vm((levels, 8, nx), f32),
        vm((levels, 8, nx), f32), vm((levels, 8, nx), f32),
        vm((ny, 128), f32),
        vm((levels, 8, nx), f32),
        vm((levels, YC, nx), f32),
        vm((levels, chunks, 2, YC, 128), f32),
        vm((chunks, nx_dev, 2, YC, 128), f32),
        vm((8 * YC, 256), f32),
        vm((2, (ny + 8) * 8, 128), f32),
        vm((2, ny * 8, 128), f32),
        vm((2, ny * 8, 128), f32),
        vm((2, ny * 8, 128), f32),
        vm((2, 8, 128), f32), vm((2, 8, 128), f32), vm((2, 8, 128), f32),
        vm((ny_dev // 2, 2, 8, 128), f32),
        vm((2, 8, 128), f32), vm((2, 8, 128), f32),
        vm((nx_dev, chunks, 2, YC, 128), f32),
        vm((chunks, levels, 2, YC, 128), f32),
        vm((nx_dev, 8, 128), f32),
        vm((128, 128), f32),
        dma((8,)), dma((4,)), dma((4,)),
        dma((chunks, nx_dev)), dma((chunks, nx_dev)), dma((chunks,)),
        dma((3,)), dma((3,)),
        dma((chunks, nx_dev)), dma((chunks, nx_dev)), dma((chunks + 1,)),
        dma((nx_dev,)), dma((nx_dev,)), pltpu.SemaphoreType.REGULAR((3,)),
    ]
    mid = pl.pallas_call(
        functools.partial(kernel, nx_dev, ny_dev),
        out_shape=(
            out,
            jax.ShapeDtypeStruct((levels, ny + 8, nx), f32),
            out,
            out,
            out,
            jax.ShapeDtypeStruct((levels, 8, 128), f32),
            jax.ShapeDtypeStruct((64, 128), f32),
            jax.ShapeDtypeStruct((56, 256), f32),
        ),
        in_specs=[hbm] * 8,
        out_specs=(vmem,) * 8,
        scratch_shapes=scratch,
        compiler_params=pltpu.CompilerParams(
            collective_id=0, has_side_effects=True, vmem_limit_bytes=36 << 20
        ),
        name="substep",
    )(*(
        pltpu.with_memory_space_constraint(a, pltpu.HBM)
        for a in (density, thickness, jnp.asarray(tab), u_face, v_face, w_face, theta_field, jnp.asarray(mats))
    ))
    return pl.pallas_call(
        finish,
        out_shape=(out,) * 5,
        in_specs=[vmem] * 8,
        out_specs=(hbm,) * 5,
        scratch_shapes=[
            vm(full, f32), vm(full, f32), vm(full, f32),
            vm((128, 128), f32), vm((levels, 8, 128), f32), dma((1,)), dma((4, levels)),
        ],
        compiler_params=pltpu.CompilerParams(vmem_limit_bytes=24 << 20),
        name="finish",
    )(*mid)


def solution(mesh):
    spec = P(None, "gy", "gx")
    return jax.shard_map(
        per_device,
        mesh=mesh,
        in_specs=(spec, spec, spec, spec, P(), P()),
        out_specs=(spec,) * 5,
        check_vma=False,
    )
```

```python
import functools

import jax
import jax.numpy as jnp
import numpy as np
from jax import lax
from jax.experimental import pallas as pl
from jax.experimental.pallas import tpu as pltpu
from jax.sharding import PartitionSpec as P

DT = 0.2
f32 = jnp.float32
bf16 = jnp.bfloat16
MESH = pl.DeviceIdType.MESH
C1, C2, C3 = float(np.cos(np.pi / 8)), float(np.cos(np.pi / 4)), float(np.cos(3 * np.pi / 8))
YC = 16


def split_bf16(a):
    hi = a.astype(jnp.bfloat16)
    lo = (a - hi.astype(np.float64)).astype(jnp.bfloat16)
    return hi, lo


@functools.cache
def tables():
    n_x = 2048
    l = np.arange(128)
    n = np.arange(128)

    def cas(t):
        return np.cos(t) + np.sin(t)

    cos = np.cos(2 * np.pi * np.outer(l, n) / 128)
    sin = np.sin(2 * np.pi * np.outer(l, n) / 128)
    zero = np.zeros((128, 128))
    fw = np.block([[cos, -sin], [sin, cos]])
    b0 = cas(2 * np.pi * np.outer(l, n) / 128)
    b8 = cas(2 * np.pi * np.outer(l, 16 * n + 8) / n_x)
    fb = np.block([[b0, zero], [zero, b8]])
    mats = []
    for m in (fw, fb, fw.T * (2 / n_x), fb.T * (1 / n_x)):
        mats.extend(split_bf16(m))
    mats = np.stack(mats)
    tw = np.arange(8)[:, None] * l[None, :] * (2 * np.pi / n_x)
    k_lo = 16 * n[None, :] + np.arange(8)[:, None]
    k_hi = k_lo.copy()
    k_hi[0] += 8
    tab = np.concatenate(
        [np.cos(tw), np.sin(tw), 4 * np.sin(np.pi * k_lo / n_x) ** 2, 4 * np.sin(np.pi * k_hi / n_x) ** 2]
    ).astype(np.float32)
    return mats, tab


def fwd16(x):
    s = [x[q] + x[q + 8] for q in range(8)]
    d = [x[q] - x[q + 8] for q in range(8)]
    t = [s[q] + s[q + 4] for q in range(4)]
    e = [s[q] - s[q + 4] for q in range(4)]
    t02, t13 = t[0] + t[2], t[1] + t[3]
    re, im = {}, {}
    y0, y8 = t02 + t13, t02 - t13
    re[4], im[4] = t[0] - t[2], t[3] - t[1]
    a, b = C2 * (e[1] - e[3]), C2 * (e[1] + e[3])
    re[2], re[6] = e[0] + a, e[0] - a
    im[2], im[6] = -(e[2] + b), e[2] - b
    u = [None] + [d[q] - d[8 - q] for q in (1, 2, 3)]
    v = [None] + [d[q] + d[8 - q] for q in (1, 2, 3)]
    g = C2 * u[2]
    g1, g2 = d[0] + g, d[0] - g
    h1, h2 = C1 * u[1] + C3 * u[3], C3 * u[1] - C1 * u[3]
    re[1], re[7], re[3], re[5] = g1 + h1, g1 - h1, g2 + h2, g2 - h2
    k = C2 * v[2]
    k1, k2 = k + d[4], k - d[4]
    m1, m2 = C3 * v[1] + C1 * v[3], C1 * v[1] - C3 * v[3]
    im[1], im[7], im[3], im[5] = -(m1 + k1), k1 - m1, -(m2 + k2), k2 - m2
    return y0, y8, re, im


def inv16(a0, a8, zr, zi):
    p1, m1, p3, m3 = zr[1] + zr[7], zr[1] - zr[7], zr[3] + zr[5], zr[3] - zr[5]
    r1, s1, r3, s3 = zi[1] + zi[7], zi[1] - zi[7], zi[3] + zi[5], zi[3] - zi[5]
    o = [None] * 8
    o[0] = p1 + p3
    o[4] = s3 - s1
    cs = [None, C1 * m1 + C3 * m3, C2 * (p1 - p3), C3 * m1 - C1 * m3]
    sn = [None, C3 * r1 + C1 * r3, C2 * (s1 + s3), C1 * r1 - C3 * r3]
    for q in (1, 2, 3):
        o[q] = cs[q] - sn[q]
        o[8 - q] = -cs[q] - sn[q]
    ap, am = a0 + a8, a0 - a8
    g = [ap + zr[4], am - zi[4], ap - zr[4], am + zi[4]]
    w1, w2 = C2 * (zr[2] - zr[6]), C2 * (zi[2] + zi[6])
    h = [zr[2] + zr[6], w1 - w2, zi[6] - zi[2], -w1 - w2]
    ev = [g[q] + h[q] for q in range(4)] + [g[q] - h[q] for q in range(4)]
    return [ev[q] + o[q] for q in range(8)] + [ev[q] - o[q] for q in range(8)]


def dot3(x, hi, lo):
    xh = x.astype(bf16)
    xl = (x - xh.astype(f32)).astype(bf16)
    out = jnp.dot(xh, hi, preferred_element_type=f32)
    out += jnp.dot(xl, hi, preferred_element_type=f32)
    out += jnp.dot(xh, lo, preferred_element_type=f32)
    return out


def flux(qm2, qm1, q0, q1, q2, q3, c):
    s = 37.0 * (q0 + q1) - 8.0 * (qm1 + q2) + (qm2 + q3)
    d = 10.0 * (q1 - q0) - 5.0 * (q2 - qm1) + (q3 - qm2)
    return c * s - jnp.abs(c) * d


def roll(x, shift, axis):
    n = x.shape[axis]
    shift = shift % n
    return x if shift == 0 else pltpu.roll(x, shift, axis)


def lanes(shape):
    return lax.broadcasted_iota(jnp.int32, shape, len(shape) - 1)


def rows_of(shape):
    return lax.broadcasted_iota(jnp.int32, shape, 0)


def kernel(
    nx_dev, ny_dev,
    den_hbm, thk_hbm, tab_hbm, u_hbm, v_hbm, w_hbm, th_hbm, mats_hbm,
    U, V, WS, tn_ref, p_ref, XR, TI,
    den_ref, thk_ref, tab_ref, COEF, W, TH, MATS, TF, LAM,
    PE_S, PW_S, PE_R, PW_R, YN_S, YS_S, YN_R, YS_R, FPK, FYP,
    SRC, TX1, RX1, Z, S, SA, SB, PWR, IFS, IFR, CBS, CBR, INS, INR, TX2, RX2, X2, EW,
    in_sem, hs_sem, hr_sem, s1_sem, r1_sem, l1_sem, is_sem, ir_sem, s2_sem, r2_sem, l2_sem,
    sx_sem, rx_sem,
):
    gx = lax.axis_index("gx")
    gy = lax.axis_index("gy")
    levels, ny, nx = u_hbm.shape
    chunks = ny // YC

    def px(t):
        return lax.rem(gx + t, nx_dev)

    def py(t):
        return lax.rem(gy + t, ny_dev)

    n_chips = ny_dev // 2
    chip, core = gy // 2, lax.rem(gy, 2)

    def chip_at(t):
        return 2 * lax.rem(chip + t, n_chips) + core

    mid = pl.ds(8, ny)
    small = [
        pltpu.make_async_copy(den_hbm, den_ref, in_sem.at[5]),
        pltpu.make_async_copy(thk_hbm, thk_ref, in_sem.at[6]),
        pltpu.make_async_copy(tab_hbm, tab_ref, in_sem.at[7]),
    ]
    loads = [
        pltpu.make_async_copy(w_hbm, W.at[:, mid, :], in_sem.at[0]),
        pltpu.make_async_copy(th_hbm, TH.at[:, mid, :], in_sem.at[1]),
        pltpu.make_async_copy(u_hbm, U, in_sem.at[2]),
        pltpu.make_async_copy(v_hbm, V.at[:, mid, :], in_sem.at[3]),
        pltpu.make_async_copy(mats_hbm, MATS, in_sem.at[4]),
    ]
    for cp in small + loads:
        cp.start()

    barrier = pltpu.get_barrier_semaphore()
    for t in range(1, nx_dev):
        pl.semaphore_signal(barrier, inc=1, device_id={"gx": px(t)}, device_id_type=MESH)

    for t in (1, ny_dev - 1):
        pl.semaphore_signal(barrier, inc=1, device_id={"gy": py(t)}, device_id_type=MESH)
    for t in range(1, n_chips):
        pl.semaphore_signal(barrier, inc=1, device_id={"gy": chip_at(t)}, device_id_type=MESH)

    for cp in small:
        cp.wait()

    r8 = rows_of((8, 128))
    j8 = lax.rem(lanes((8, 128)), 8)
    den = jnp.zeros((8, 128), f32)
    thk = jnp.zeros((8, 128), f32)
    for k in range(levels):
        den = jnp.where(r8 == k, den_ref[k], den)
        thk = jnp.where(r8 == k, thk_ref[k], thk)

    def lift(a):
        return jnp.where(r8 == 7, a, roll(a, -1, 0))

    def below(a):
        return jnp.where(r8 == 0, 0.0, roll(a, 1, 0))

    lden = lift(den)
    fd = (den + lden) / 2.0
    fs = (thk + lift(thk)) / 2.0
    mass = den * thk
    zw = (DT / 60.0) / (fd * fs)
    zt = (DT / 60.0) / mass
    sc = (1.0 / DT) / mass
    coefs = [lden * zw, below(lden) * zw, fd * zt, below(fd) * zt, fd * sc, below(fd) * sc, DT / fs]
    for i, a in enumerate(coefs):
        COEF[i * 8 : i * 8 + 8, :] = jnp.concatenate([a, a], axis=1)

    cond = fd / fs
    diag = jnp.sqrt(cond / mass)
    off = -jnp.sqrt(cond / lift(mass))
    b_mat = jnp.where(j8 == r8, diag, jnp.where(j8 == r8 + 1, off, 0.0))
    q_mat = jnp.where(j8 == r8, 1.0, 0.0)
    pairs = [
        (4, j8 < 4),
        (1, lax.rem(j8, 2) == 0), (1, lax.rem(j8, 2) == 1),
        (3, lax.rem(j8, 2) == 0), (3, lax.rem(j8, 2) == 1),
        (2, lax.rem(j8, 4) < 2), (2, lax.rem(j8, 4) >= 2),
    ]

    def total(x):
        return ((x[0] + x[1]) + (x[2] + x[3])) + ((x[4] + x[5]) + (x[6] + x[7]))

    def partner(x, o, ahead):
        if o == 4:
            return roll(x, 4, 1)
        return jnp.where(ahead, roll(x, -o, 1), roll(x, o, 1))

    def sweep(_, carry):
        b, q = list(carry[:8]), list(carry[8:])
        for o, ahead in pairs:
            bp = [partner(x, o, ahead) for x in b]
            al = total([x * x for x in b])
            ap = total([x * x for x in bp])
            g = total([x * y for x, y in zip(b, bp)])
            d = ap - al
            h2 = d * d + 4.0 * g * g
            ok = h2 > 1e-30
            rh = lax.rsqrt(jnp.where(ok, h2, 1.0))
            c2 = 0.5 + 0.5 * jnp.abs(d) * rh
            rc = lax.rsqrt(c2)
            sg = jnp.where(d > 0.0, g, jnp.where(d < 0.0, -g, jnp.where(ahead, g, -g)))
            c = jnp.where(ok, c2 * rc, 1.0)
            s = jnp.where(ok, sg * rh * rc, 0.0)
            qp = [partner(x, o, ahead) for x in q]
            b = [c * x - s * y for x, y in zip(b, bp)]
            q = [c * x - s * y for x, y in zip(q, qp)]
        return (*b, *q)

    start = [jnp.broadcast_to(m[k : k + 1], (8, 128)) for m in (b_mat, q_mat) for k in range(8)]
    got = lax.fori_loop(0, 5, sweep, tuple(start))
    norm = 1.0 / total([x * x for x in got[8:]])
    lam = total([x * x for x in got[:8]]) * norm
    unit = jnp.sqrt(norm)
    q_mat = jnp.zeros((8, 128), f32)
    for k in range(8):
        q_mat = jnp.where(r8 == k, got[8 + k] * unit, q_mat)
    root = jnp.sqrt(mass)
    qf = q_mat * root
    qi = q_mat / root
    for j in range(8):
        TF[j * 8 : j * 8 + 8, :] = jnp.broadcast_to(qf[:, j : j + 1], (8, 128))
        TI[j * 8 : j * 8 + 8, :] = jnp.broadcast_to(qi[:, j : j + 1], (8, 128))
        LAM[j] = jnp.broadcast_to(lam[:, j : j + 1], (8, 128))

    for cp in loads[:4]:
        cp.wait()
    lane_c = lanes((YC, 128))

    @pl.loop(0, chunks)
    def _(c):
        y0 = pl.multiple_of(c * YC, YC)
        east = jnp.zeros((YC, 128), f32)
        west = jnp.zeros((YC, 128), f32)
        for k in range(levels):
            o = 16 * k
            rows = pl.ds(y0 + 8, YC)
            wl, wr = W[k, rows, 0:128], W[k, rows, 128:256]
            tl, tr = TH[k, rows, 0:128], TH[k, rows, 128:256]
            ur = U[k, pl.ds(y0, YC), 128:256]
            east = jnp.where((lane_c >= o) & (lane_c < o + 3), roll(wr, o - 125, 1), east)
            east = jnp.where((lane_c >= o + 3) & (lane_c < o + 6), roll(tr, o + 3 - 125, 1), east)
            east = jnp.where(lane_c == o + 6, roll(ur, o + 6 - 127, 1), east)
            west = jnp.where((lane_c >= o) & (lane_c < o + 3), roll(wl, o, 1), west)
            west = jnp.where((lane_c >= o + 3) & (lane_c < o + 6), roll(tl, o + 3, 1), west)
        PE_S[pl.ds(y0, YC), :] = east
        PW_S[pl.ds(y0, YC), :] = west

    for k in range(levels):
        a, b, c = W[k, ny : ny + 8, :], TH[k, ny : ny + 8, :], V[k, ny : ny + 8, :]
        row = rows_of((8, nx))
        YN_S[k] = jnp.where(row < 3, roll(a, 3, 0), jnp.where(row < 6, roll(b, 6, 0), roll(c, 7, 0)))
        a, b = W[k, 8:16, :], TH[k, 8:16, :]
        YS_S[k] = jnp.where(row < 3, a, roll(b, 3, 0))

    pl.semaphore_wait(barrier, nx_dev - 1 + 2 + n_chips - 1)
    halos = []
    for i, (src, dst, where) in enumerate(
        [
            (PE_S, PE_R, {"gx": px(1)}),
            (PW_S, PW_R, {"gx": px(nx_dev - 1)}),
            (YN_S, YN_R, {"gy": py(1)}),
            (YS_S, YS_R, {"gy": py(ny_dev - 1)}),
        ]
    ):
        cp = pltpu.make_async_remote_copy(
            src_ref=src, dst_ref=dst, send_sem=hs_sem.at[i], recv_sem=hr_sem.at[i],
            device_id=where, device_id_type=MESH,
        )
        cp.start()
        halos.append(cp)

    def nxt(k):
        return min(k + 1, levels - 1)

    def z_part(field, k, rows, w, fz_below, zi):
        zq = [field[min(max(k + s, 0), levels - 1), rows, :] for s in range(-2, 4)]
        fz = flux(*zq, w)
        tend = COEF[zi + k : zi + k + 1, :] * fz
        if k > 0:
            tend = tend - COEF[zi + 8 + k : zi + 9 + k, :] * fz_below
        return tend, fz

    @pl.loop(0, chunks)
    def _(c):
        y0 = pl.multiple_of(c * YC, YC)
        rows = pl.ds(y0 + 8, YC)
        fz = None
        for k in range(levels):
            w, w1 = W[k, rows, :], W[nxt(k), rows, :]
            tend, fz = z_part(W, k, rows, (w + w1) / 2.0, fz, 0)
            WS[k, pl.ds(y0, YC), :] = w - tend + (0.5 * DT) * (TH[k, rows, :] + TH[nxt(k), rows, :])

    for cp in halos:
        cp.wait()

    for k in range(levels):
        n8, s8 = YN_R[k], YS_R[k]
        W[k, 0:8, :] = roll(n8, 5, 0)
        TH[k, 0:8, :] = roll(n8, 2, 0)
        V[k, 0:8, :] = roll(n8, 1, 0)
        W[k, ny + 8 : ny + 16, :] = s8
        TH[k, ny + 8 : ny + 16, :] = roll(s8, 5, 0)

    lane_n = lanes((ny, 128))
    ph, po = PE_R[...], PW_S[...]
    lane_m = lax.rem(lane_n, 16)
    u_th = roll(ph, -3, 1)
    u_top = jnp.where(lane_n >= 112, roll(ph, -6, 1), roll(ph, -22, 1))
    u_w = (roll(ph, -6, 1) + u_top) / 2.0
    FPK[...] = flux(
        ph, roll(ph, -1, 1), roll(ph, -2, 1), po, roll(po, -1, 1), roll(po, -2, 1),
        jnp.where(lane_m == 0, u_w, u_th),
    )

    def y_shifts(block, n):
        return [roll(block, -s, 0)[8 : 8 + n] if s else block[8 : 8 + n] for s in range(-2, 4)]

    def south_flux(field, first, lifted):
        for k in range(levels):
            block = field[k, 0:16, :]
            qs = [roll(block, -s, 0)[0:8] for s in range(-2, 4)]
            c = V[k, 0:8, :]
            if lifted:
                c = (c + V[nxt(k), 0:8, :]) / 2.0
            FYP[k] = flux(*qs, c)

    def horizontal(field, k, y0, extra, lifted):
        o = 16 * k + extra
        rows = pl.ds(y0 + 8, YC)
        cen = pl.ds(y0, YC)
        block = field[k, pl.ds(y0, YC + 16), :]
        q = block[8 : 8 + YC]
        left, right = q[:, :128], q[:, 128:]
        pe, pw = PW_R[cen, :], PE_R[cen, :]
        ls, rs = [], []
        for s in range(-2, 4):
            if s == 0:
                ls.append(left)
                rs.append(right)
                continue
            a, b = roll(left, -s, 1), roll(right, -s, 1)
            if s > 0:
                ls.append(jnp.where(lane_c < 128 - s, a, b))
                rs.append(jnp.where(lane_c < 128 - s, b, roll(pe, -s - o, 1)))
            else:
                ls.append(jnp.where(lane_c >= -s, a, roll(pw, -s - 3 - o, 1)))
                rs.append(jnp.where(lane_c >= -s, b, a))
        u, v = U[k, cen, :], V[k, rows, :]
        if lifted:
            u = (u + U[nxt(k), cen, :]) / 2.0
            v = (v + V[nxt(k), rows, :]) / 2.0
        fl = flux(*ls, u[:, :128])
        fr = flux(*rs, u[:, 128:])
        fl_roll = roll(fl, 1, 1)
        wl = jnp.where(lane_c >= 1, fl_roll, roll(FPK[cen, :], -o, 1))
        wr = jnp.where(lane_c >= 1, roll(fr, 1, 1), fl_roll)
        div = jnp.concatenate([fl - wl, fr - wr], axis=1)
        fy = flux(*y_shifts(block, YC), v)
        prev = roll(jnp.concatenate([FYP[k], fy], axis=0), 1, 0)[8:]
        FYP[k] = fy[YC - 8 :]
        div = div + (fy - prev)
        return (-DT / 60.0) * div

    def send(src, dst, s_sem, r_sem, who):
        return pltpu.make_async_remote_copy(
            src_ref=src, dst_ref=dst, send_sem=s_sem, recv_sem=r_sem,
            device_id=who, device_id_type=MESH,
        )

    south_flux(W, 0, True)

    @pl.loop(0, chunks)
    def _(c):
        y0 = pl.multiple_of(c * YC, YC)
        cen = pl.ds(y0, YC)
        star_below = None
        for k in range(levels):
            star = WS[k, cen, :] + horizontal(W, k, y0, 0, True)
            WS[k, cen, :] = star
            u = U[k, cen, :]
            ul = roll(u[:, :128], 1, 1)
            uw = jnp.where(lane_c >= 1, ul, roll(PE_R[cen, :], -(16 * k + 6), 1))
            ue = jnp.where(lane_c >= 1, roll(u[:, 128:], 1, 1), ul)
            vb = V[k, pl.ds(y0, YC + 8), :]
            dv = (vb - roll(vb, 1, 0))[8:]
            src = (u - jnp.concatenate([uw, ue], axis=1) + dv) * (1.0 / DT)
            src = src + COEF[32 + k : 33 + k, :] * star
            if k > 0:
                src = src - COEF[40 + k : 41 + k, :] * star_below
            star_below = star
            SRC[k] = src
        for h in range(2):
            hs = slice(128 * h, 128 * h + 128)
            col = [SRC[k, :, hs] for k in range(levels)]
            for j in range(levels):
                acc = TF[j * 8 : j * 8 + 1, :] * col[0]
                for k in range(1, levels):
                    acc = acc + TF[j * 8 + k : j * 8 + k + 1, :] * col[k]
                TX1[j, c, h] = acc
        pltpu.make_async_copy(TX1.at[gx, c], RX1.at[c, gx], l1_sem.at[c]).start()
        for t in range(1, nx_dev):
            g = px(t)
            send(TX1.at[g, c], RX1.at[c, gx], s1_sem.at[c, t], r1_sem.at[c, gx], {"gx": g}).start()

    south_flux(TH, 0, False)

    @pl.loop(0, chunks)
    def _(c):
        y0 = pl.multiple_of(c * YC, YC)
        fz = None
        for k in range(levels):
            rows = pl.ds(y0 + 8, YC)
            tend, fz = z_part(TH, k, rows, W[k, rows, :], fz, 16)
            tn_ref[k, pl.ds(y0, YC), :] = TH[k, rows, :] - tend + horizontal(TH, k, y0, 3, False)

    lam_g = LAM[gx]
    rate, scale = [], []
    for h in range(2):
        mu = lam_g + tab_ref[16 + 8 * h : 24 + 8 * h, :]
        rt = jnp.sqrt(mu * mu + 4.0 * mu)
        rate.append(2.0 / (2.0 + mu + rt))
        scale.append(-1.0 / rt)

    loads[4].wait()

    def x_forward(c, carry):
        y0 = pl.multiple_of(c * YC, YC)
        pltpu.make_async_copy(TX1.at[gx, c], RX1.at[c, gx], l1_sem.at[c]).wait()
        for t in range(1, nx_dev):
            g = px(t)
            send(TX1.at[g, c], RX1.at[c, g], s1_sem.at[c, t], r1_sem.at[c, g], {"gx": g}).wait_recv()
        for i in range(YC // 8):
            sub = slice(8 * i, 8 * i + 8)
            x = [RX1[c, q // 2, q % 2, sub, :] for q in range(16)]
            y_0, y_8, re, im = fwd16(x)
            Z[8 * i : 8 * i + 8, 0:128] = y_0
            Z[8 * i : 8 * i + 8, 128:256] = y_8
            for m in range(1, 8):
                co, si = tab_ref[m : m + 1, :], tab_ref[8 + m : 9 + m, :]
                at = m * YC + 8 * i
                Z[at : at + 8, 0:128] = re[m] * co + im[m] * si
                Z[at : at + 8, 128:256] = im[m] * co - re[m] * si
        o0 = dot3(Z[0:YC, :], MATS[2], MATS[3])
        om = dot3(Z[YC : 8 * YC, :], MATS[0], MATS[1])
        for m in range(8):
            val = o0 if m == 0 else om[(m - 1) * YC : m * YC]
            for h in range(2):
                S[h, pl.ds(y0 * 8 + m, YC, stride=8), :] = val[:, 128 * h : 128 * h + 128]
        a0, a1, b0, b1, p0, p1 = carry
        for i in range(YC):
            at = pl.ds(y0 * 8 + 8 * i, 8)
            f0, f1 = S[0, at, :], S[1, at, :]
            a0, a1 = f0 + rate[0] * a0, f1 + rate[1] * a1
            b0, b1 = b0 + p0 * f0, b1 + p1 * f1
            SA[0, at, :], SA[1, at, :] = a0, a1
            PWR[0, at, :], PWR[1, at, :] = p0, p1
            p0, p1 = p0 * rate[0], p1 * rate[1]
        return a0, a1, b0, b1, p0, p1

    zero = jnp.zeros((8, 128), f32)
    one = jnp.ones((8, 128), f32)
    a0, a1, b0, b1, p0, p1 = lax.fori_loop(0, chunks, x_forward, (zero, zero, zero, zero, one, one))

    first = core == 0
    whole = [p0, p1]
    mine = []
    for h, (a, b) in enumerate([(a0, b0), (a1, b1)]):
        IFS[h] = jnp.where(first, a, b)
        mine.append(jnp.where(first, b, a))
    pair = {"gy": gy + 1 - 2 * core}
    swap = send(IFS, IFR, is_sem.at[0], ir_sem.at[0], pair)
    swap.start()
    swap.wait()
    for h in range(2):
        CBS[h] = mine[h] + whole[h] * IFR[h]
    sign = 2 * core - 1
    for t in (4, 12, 11, 5, 3, 13, 10, 6, 2, 14, 8, 9, 7, 1, 15):
        dev = 2 * lax.rem(chip + t * sign + n_chips, n_chips) + core
        send(CBS, CBR.at[t], is_sem.at[1], ir_sem.at[1], {"gy": dev}).start()

    def back(i, carry):
        y = ny - 1 - i
        at = pl.ds(pl.multiple_of(y * 8, 8), 8)
        out = []
        for h in range(2):
            b = rate[h] * carry[h]
            SB[h, at, :] = SA[h, at, :] + b
            out.append(S[h, at, :] + b)
        return tuple(out)

    lax.fori_loop(0, ny, back, (zero, zero), unroll=8)

    others = pl.ds(1, n_chips - 1)
    send(CBR.at[others], CBR.at[others], is_sem.at[1], ir_sem.at[1], pair).wait()
    into = []
    for h in range(2):
        ratio = whole[h] * whole[h]
        acc = CBS[h]
        for t in range(n_chips - 1, 0, -1):
            acc = CBR[t, h] + ratio * acc
        full = ratio
        n = 1
        while n < n_chips:
            full = full * full
            n *= 2
        into.append(acc / (1.0 - full))
        INS[h] = into[h]
    swap = send(INS, INR, is_sem.at[2], ir_sem.at[2], pair)
    swap.start()
    swap.wait()
    ain, bin_ = [], []
    for h in range(2):
        own = IFR[h] + whole[h] * into[h]
        ain.append(jnp.where(first, INR[h], own))
        bin_.append(jnp.where(first, own, INR[h]))
    ra = [rate[h] * ain[h] for h in range(2)]
    rb = [rate[h] * bin_[h] for h in range(2)]

    def correct(y0, n):
        for i in range(n):
            at = pl.ds(y0 * 8 + 8 * i, 8)
            mirror = pl.ds((ny - 1 - i) * 8 - y0 * 8, 8)
            for h in range(2):
                S[h, at, :] = scale[h] * (SB[h, at, :] + PWR[h, at, :] * ra[h] + PWR[h, mirror, :] * rb[h])

    end = slice((ny - 1) * 8, ny * 8)
    for h in range(2):
        last = SA[h, end, :] + PWR[h, end, :] * ra[h]
        S[h, ny * 8 : ny * 8 + 8, :] = scale[h] * (rate[h] * last + bin_[h])
        S[h, ny * 8 + 8 : ny * 8 + 64, :] = jnp.zeros((56, 128), f32)

    def x_inverse(y0, n, put):
        for m in range(8):
            for h in range(2):
                Z[m * n : m * n + n, 128 * h : 128 * h + 128] = S[h, pl.ds(y0 * 8 + m, n, stride=8), :]
        o0 = dot3(Z[0:n, :], MATS[6], MATS[7])
        om = dot3(Z[n : 8 * n, :], MATS[4], MATS[5])
        Z[0:n, :] = o0
        Z[n : 8 * n, :] = om
        for i in range(n // 8):
            zr, zi = {}, {}
            for m in range(1, 8):
                co, si = tab_ref[m : m + 1, :], tab_ref[8 + m : 9 + m, :]
                at = m * n + 8 * i
                a, b = Z[at : at + 8, 0:128], Z[at : at + 8, 128:256]
                zr[m] = a * co - b * si
                zi[m] = a * si + b * co
            put(i, inv16(Z[8 * i : 8 * i + 8, 0:128], Z[8 * i : 8 * i + 8, 128:256], zr, zi))

    lane_8 = lanes((8, 128))

    @pl.loop(0, chunks)
    def _(c):
        y0 = pl.multiple_of(c * YC, YC)

        def put(i, x):
            edge = jnp.zeros((8, 128), f32)
            for q in range(16):
                TX2[q // 2, c, q % 2, 8 * i : 8 * i + 8, :] = x[q]
            for d in range(nx_dev):
                edge = jnp.where(lane_8 == d, roll(x[(2 * d + 2) % 16], d, 1), edge)
            EW[pl.ds(y0 + 8 * i, 8), :] = edge

        correct(y0, YC)
        x_inverse(y0, YC, put)
        pltpu.make_async_copy(TX2.at[gx, c], RX2.at[c, gx], l2_sem.at[c]).start()
        for t in range(1, nx_dev):
            g = px(t)
            send(TX2.at[g, c], RX2.at[c, gx], s2_sem.at[c, t], r2_sem.at[c, gx], {"gx": g}).start()

    EW[ny:128, :] = jnp.zeros((128 - ny, 128), f32)
    ewt = jnp.transpose(EW[...])
    row8 = rows_of((8, 128))

    def put_north(i, x):
        for d in range(nx_dev):
            e = jnp.broadcast_to(ewt[d : d + 1, :], (8, 128))
            n0 = jnp.broadcast_to(x[2 * d][0:1], (8, 128))
            n1 = jnp.broadcast_to(x[2 * d + 1][0:1], (8, 128))
            X2[d] = jnp.where(row8 == 0, n0, jnp.where(row8 == 1, n1, e))

    x_inverse(ny, 8, put_north)
    pltpu.make_async_copy(X2.at[gx], XR.at[gx], l2_sem.at[chunks]).start()
    for t in range(1, nx_dev):
        g = px(t)
        send(X2.at[g], XR.at[gx], sx_sem.at[t], rx_sem.at[gx], {"gx": g}).start()

    @pl.loop(0, chunks)
    def _(c):
        pltpu.make_async_copy(TX2.at[gx, c], RX2.at[c, gx], l2_sem.at[c]).wait()
        for t in range(1, nx_dev):
            g = px(t)
            send(TX2.at[g, c], RX2.at[c, g], s2_sem.at[c, t], r2_sem.at[c, g], {"gx": g}).wait_recv()
        cen = pl.ds(pl.multiple_of(c * YC, YC), YC)
        for h in range(2):
            col = [RX2[c, j, h] for j in range(levels)]
            for k in range(levels):
                acc = TI[k : k + 1, :] * col[0]
                for j in range(1, levels):
                    acc = acc + TI[j * 8 + k : j * 8 + k + 1, :] * col[j]
                p_ref[k, cen, 128 * h : 128 * h + 128] = acc
        for k in range(levels):
            g = COEF[48 + k : 49 + k, :]
            step = p_ref[k + 1, cen, :] - p_ref[k, cen, :] if k + 1 < levels else -p_ref[k, cen, :]
            WS[k, cen, :] = WS[k, cen, :] - g * step

    pltpu.make_async_copy(X2.at[gx], XR.at[gx], l2_sem.at[chunks]).wait()
    for t in range(1, nx_dev):
        g = px(t)
        send(X2.at[g], XR.at[g], sx_sem.at[t], rx_sem.at[g], {"gx": g}).wait_recv()

    @pl.loop(0, chunks)
    def _(c):
        for t in range(1, nx_dev):
            g = px(t)
            send(TX1.at[g, c], RX1.at[c, g], s1_sem.at[c, t], r1_sem.at[c, g], {"gx": g}).wait_send()
            send(TX2.at[g, c], RX2.at[c, g], s2_sem.at[c, t], r2_sem.at[c, g], {"gx": g}).wait_send()

    for t in range(1, nx_dev):
        g = px(t)
        send(X2.at[g], XR.at[g], sx_sem.at[t], rx_sem.at[g], {"gx": g}).wait_send()


def finish(
    U, V, WS, tn_ref, p_ref, XR, TI, un_hbm, vn_hbm, wn_hbm, tn_hbm, p_hbm,
    un_ref, vn_ref, EC, EX, tn_sem, out_sem,
):
    levels, ny, nx = U.shape
    theta = pltpu.make_async_copy(tn_ref, tn_hbm, tn_sem.at[0])
    theta.start()
    lane_n = lanes((ny, 128))
    row8 = rows_of((8, 128))

    def out(i, ref, hbm, k):
        return pltpu.make_async_copy(ref.at[k], hbm.at[k], out_sem.at[i, k])

    outs = [(p_ref, p_hbm), (un_ref, un_hbm), (vn_ref, vn_hbm), (WS, wn_hbm)]
    for k in range(levels):
        out(0, p_ref, p_hbm, k).start()
        out(3, WS, wn_hbm, k).start()

    east = jnp.zeros((8, 128), f32)
    for k in range(levels):
        acc = TI[k : k + 1, :] * XR[0]
        for j in range(1, levels):
            acc = acc + TI[j * 8 + k : j * 8 + k + 1, :] * XR[j]
        EX[k] = acc
        east = jnp.where(row8 == k, jnp.broadcast_to(acc[2:3, :], (8, 128)), east)
    EC[0:8, :] = east
    EC[8:128, :] = jnp.zeros((120, 128), f32)
    EC[...] = jnp.transpose(EC[...])

    for k in range(levels):
        p = p_ref[k]
        pleft, pright = p[:, :128], p[:, 128:]
        col = jnp.broadcast_to(EC[0:ny, k : k + 1], (ny, 128))
        a, b = roll(pleft, -1, 1), roll(pright, -1, 1)
        gl = jnp.where(lane_n < 127, a, b) - pleft
        gr = jnp.where(lane_n < 127, b, col) - pright
        un_ref[k] = U[k] - DT * jnp.concatenate([gl, gr], axis=1)
        out(1, un_ref, un_hbm, k).start()
        ex = EX[k]
        north = jnp.concatenate([ex[0:1, :], ex[1:2, :]], axis=1)
        shifted = roll(p, -1, 0)
        shifted = jnp.where(rows_of((ny, nx)) < ny - 1, shifted, jnp.broadcast_to(north, (ny, nx)))
        vn_ref[k] = V[k, 8 : 8 + ny, :] - DT * (shifted - p)
        out(2, vn_ref, vn_hbm, k).start()

    theta.wait()
    for k in range(levels):
        for i, (ref, hbm) in enumerate(outs):
            out(i, ref, hbm, k).wait()


def per_device(u_face, v_face, w_face, theta_field, density, thickness):
    nx_dev = lax.axis_size("gx")
    ny_dev = lax.axis_size("gy")
    levels, ny, nx = u_face.shape
    chunks = ny // YC
    mats, tab = tables()
    vm = pltpu.VMEM
    dma = pltpu.SemaphoreType.DMA
    full = (levels, ny, nx)
    out = jax.ShapeDtypeStruct(full, f32)
    hbm = pl.BlockSpec(memory_space=pltpu.HBM)
    vmem = pl.BlockSpec(memory_space=pltpu.VMEM)
    scratch = [
        pltpu.SMEM((levels,), f32), pltpu.SMEM((levels,), f32), vm((32, 128), f32),
        vm((56, 256), f32),
        vm((levels, ny + 16, nx), f32),
        vm((levels, ny + 16, nx), f32),
        vm((8, 256, 256), bf16),
        vm((64, 128), f32),
        vm((8, 8, 128), f32),
        vm((ny, 128), f32), vm((ny, 128), f32), vm((ny, 128), f32), vm((ny, 128), f32),
        vm((levels, 8, nx), f32), vm((levels, 8, nx), f32),
        vm((levels, 8, nx), f32), vm((levels, 8, nx), f32),
        vm((ny, 128), f32),
        vm((levels, 8, nx), f32),
        vm((levels, YC, nx), f32),
        vm((levels, chunks, 2, YC, 128), f32),
        vm((chunks, nx_dev, 2, YC, 128), f32),
        vm((8 * YC, 256), f32),
        vm((2, (ny + 8) * 8, 128), f32),
        vm((2, ny * 8, 128), f32),
        vm((2, ny * 8, 128), f32),
        vm((2, ny * 8, 128), f32),
        vm((2, 8, 128), f32), vm((2, 8, 128), f32), vm((2, 8, 128), f32),
        vm((ny_dev // 2, 2, 8, 128), f32),
        vm((2, 8, 128), f32), vm((2, 8, 128), f32),
        vm((nx_dev, chunks, 2, YC, 128), f32),
        vm((chunks, levels, 2, YC, 128), f32),
        vm((nx_dev, 8, 128), f32),
        vm((128, 128), f32),
        dma((8,)), dma((4,)), dma((4,)),
        dma((chunks, nx_dev)), dma((chunks, nx_dev)), dma((chunks,)),
        dma((3,)), dma((3,)),
        dma((chunks, nx_dev)), dma((chunks, nx_dev)), dma((chunks + 1,)),
        dma((nx_dev,)), dma((nx_dev,)),
    ]
    mid = pl.pallas_call(
        functools.partial(kernel, nx_dev, ny_dev),
        out_shape=(
            out,
            jax.ShapeDtypeStruct((levels, ny + 8, nx), f32),
            out,
            out,
            out,
            jax.ShapeDtypeStruct((levels, 8, 128), f32),
            jax.ShapeDtypeStruct((64, 128), f32),
        ),
        in_specs=[hbm] * 8,
        out_specs=(vmem,) * 7,
        scratch_shapes=scratch,
        compiler_params=pltpu.CompilerParams(
            collective_id=0, has_side_effects=True, vmem_limit_bytes=36 << 20
        ),
        name="substep",
    )(*(
        pltpu.with_memory_space_constraint(a, pltpu.HBM)
        for a in (density, thickness, jnp.asarray(tab), u_face, v_face, w_face, theta_field, jnp.asarray(mats))
    ))
    return pl.pallas_call(
        finish,
        out_shape=(out,) * 5,
        in_specs=[vmem] * 7,
        out_specs=(hbm,) * 5,
        scratch_shapes=[
            vm(full, f32), vm(full, f32),
            vm((128, 128), f32), vm((levels, 8, 128), f32), dma((1,)), dma((4, levels)),
        ],
        compiler_params=pltpu.CompilerParams(vmem_limit_bytes=24 << 20),
        name="finish",
    )(*mid)


def solution(mesh):
    spec = P(None, "gy", "gx")
    return jax.shard_map(
        per_device,
        mesh=mesh,
        in_specs=(spec, spec, spec, spec, P(), P()),
        out_specs=(spec,) * 5,
        check_vma=False,
    )
```

```python
import functools

import jax
import jax.numpy as jnp
import numpy as np
from jax import lax
from jax.experimental import pallas as pl
from jax.experimental.pallas import tpu as pltpu
from jax.sharding import PartitionSpec as P

DT = 0.2
f32 = jnp.float32
bf16 = jnp.bfloat16
MESH = pl.DeviceIdType.MESH
C1, C2, C3 = float(np.cos(np.pi / 8)), float(np.cos(np.pi / 4)), float(np.cos(3 * np.pi / 8))
YC = 16


def split_bf16(a):
    hi = a.astype(jnp.bfloat16)
    lo = (a - hi.astype(np.float64)).astype(jnp.bfloat16)
    return hi, lo


@functools.cache
def tables():
    n_x = 2048
    l = np.arange(128)
    n = np.arange(128)

    def cas(t):
        return np.cos(t) + np.sin(t)

    cos = np.cos(2 * np.pi * np.outer(l, n) / 128)
    sin = np.sin(2 * np.pi * np.outer(l, n) / 128)
    zero = np.zeros((128, 128))
    fw = np.block([[cos, -sin], [sin, cos]])
    b0 = cas(2 * np.pi * np.outer(l, n) / 128)
    b8 = cas(2 * np.pi * np.outer(l, 16 * n + 8) / n_x)
    fb = np.block([[b0, zero], [zero, b8]])
    mats = []
    for m in (fw, fb, fw.T * (2 / n_x), fb.T * (1 / n_x)):
        mats.extend(split_bf16(m))
    mats = np.stack(mats)
    tw = np.arange(8)[:, None] * l[None, :] * (2 * np.pi / n_x)
    k_lo = 16 * n[None, :] + np.arange(8)[:, None]
    k_hi = k_lo.copy()
    k_hi[0] += 8
    tab = np.concatenate(
        [np.cos(tw), np.sin(tw), 4 * np.sin(np.pi * k_lo / n_x) ** 2, 4 * np.sin(np.pi * k_hi / n_x) ** 2]
    ).astype(np.float32)
    return mats, tab


def fwd16(x):
    s = [x[q] + x[q + 8] for q in range(8)]
    d = [x[q] - x[q + 8] for q in range(8)]
    t = [s[q] + s[q + 4] for q in range(4)]
    e = [s[q] - s[q + 4] for q in range(4)]
    t02, t13 = t[0] + t[2], t[1] + t[3]
    re, im = {}, {}
    y0, y8 = t02 + t13, t02 - t13
    re[4], im[4] = t[0] - t[2], t[3] - t[1]
    a, b = C2 * (e[1] - e[3]), C2 * (e[1] + e[3])
    re[2], re[6] = e[0] + a, e[0] - a
    im[2], im[6] = -(e[2] + b), e[2] - b
    u = [None] + [d[q] - d[8 - q] for q in (1, 2, 3)]
    v = [None] + [d[q] + d[8 - q] for q in (1, 2, 3)]
    g = C2 * u[2]
    g1, g2 = d[0] + g, d[0] - g
    h1, h2 = C1 * u[1] + C3 * u[3], C3 * u[1] - C1 * u[3]
    re[1], re[7], re[3], re[5] = g1 + h1, g1 - h1, g2 + h2, g2 - h2
    k = C2 * v[2]
    k1, k2 = k + d[4], k - d[4]
    m1, m2 = C3 * v[1] + C1 * v[3], C1 * v[1] - C3 * v[3]
    im[1], im[7], im[3], im[5] = -(m1 + k1), k1 - m1, -(m2 + k2), k2 - m2
    return y0, y8, re, im


def inv16(a0, a8, zr, zi):
    p1, m1, p3, m3 = zr[1] + zr[7], zr[1] - zr[7], zr[3] + zr[5], zr[3] - zr[5]
    r1, s1, r3, s3 = zi[1] + zi[7], zi[1] - zi[7], zi[3] + zi[5], zi[3] - zi[5]
    o = [None] * 8
    o[0] = p1 + p3
    o[4] = s3 - s1
    cs = [None, C1 * m1 + C3 * m3, C2 * (p1 - p3), C3 * m1 - C1 * m3]
    sn = [None, C3 * r1 + C1 * r3, C2 * (s1 + s3), C1 * r1 - C3 * r3]
    for q in (1, 2, 3):
        o[q] = cs[q] - sn[q]
        o[8 - q] = -cs[q] - sn[q]
    ap, am = a0 + a8, a0 - a8
    g = [ap + zr[4], am - zi[4], ap - zr[4], am + zi[4]]
    w1, w2 = C2 * (zr[2] - zr[6]), C2 * (zi[2] + zi[6])
    h = [zr[2] + zr[6], w1 - w2, zi[6] - zi[2], -w1 - w2]
    ev = [g[q] + h[q] for q in range(4)] + [g[q] - h[q] for q in range(4)]
    return [ev[q] + o[q] for q in range(8)] + [ev[q] - o[q] for q in range(8)]


def dot3(x, hi, lo):
    xh = x.astype(bf16)
    xl = (x - xh.astype(f32)).astype(bf16)
    out = jnp.dot(xh, hi, preferred_element_type=f32)
    out += jnp.dot(xl, hi, preferred_element_type=f32)
    out += jnp.dot(xh, lo, preferred_element_type=f32)
    return out


def flux(qm2, qm1, q0, q1, q2, q3, c):
    s = 37.0 * (q0 + q1) - 8.0 * (qm1 + q2) + (qm2 + q3)
    d = 10.0 * (q1 - q0) - 5.0 * (q2 - qm1) + (q3 - qm2)
    return c * s - jnp.abs(c) * d


def roll(x, shift, axis):
    n = x.shape[axis]
    shift = shift % n
    return x if shift == 0 else pltpu.roll(x, shift, axis)


def lanes(shape):
    return lax.broadcasted_iota(jnp.int32, shape, len(shape) - 1)


def rows_of(shape):
    return lax.broadcasted_iota(jnp.int32, shape, 0)


def kernel(
    nx_dev, ny_dev,
    den_hbm, thk_hbm, tab_hbm, u_hbm, v_hbm, w_hbm, th_hbm, mats_hbm,
    U, V, WS, tn_ref, p_ref, XR, TI,
    den_ref, thk_ref, tab_ref, COEF, W, TH, MATS, TF, LAM,
    PE_S, PW_S, PE_R, PW_R, YN_S, YS_S, YN_R, YS_R, FPK, FYP,
    SRC, TX1, RX1, Z, S, SA, SB, PWR, IFS, IFR, CBS, CBR, INS, INR, TX2, RX2, X2, EW,
    in_sem, hs_sem, hr_sem, s1_sem, r1_sem, l1_sem, is_sem, ir_sem, s2_sem, r2_sem, l2_sem,
    sx_sem, rx_sem,
):
    gx = lax.axis_index("gx")
    gy = lax.axis_index("gy")
    levels, ny, nx = u_hbm.shape
    chunks = ny // YC

    def px(t):
        return lax.rem(gx + t, nx_dev)

    def py(t):
        return lax.rem(gy + t, ny_dev)

    n_chips = ny_dev // 2
    chip, core = gy // 2, lax.rem(gy, 2)

    def chip_at(t):
        return 2 * lax.rem(chip + t, n_chips) + core

    mid = pl.ds(8, ny)
    small = [
        pltpu.make_async_copy(den_hbm, den_ref, in_sem.at[5]),
        pltpu.make_async_copy(thk_hbm, thk_ref, in_sem.at[6]),
        pltpu.make_async_copy(tab_hbm, tab_ref, in_sem.at[7]),
    ]
    loads = [
        pltpu.make_async_copy(w_hbm, W.at[:, mid, :], in_sem.at[0]),
        pltpu.make_async_copy(th_hbm, TH.at[:, mid, :], in_sem.at[1]),
        pltpu.make_async_copy(u_hbm, U, in_sem.at[2]),
        pltpu.make_async_copy(v_hbm, V.at[:, mid, :], in_sem.at[3]),
        pltpu.make_async_copy(mats_hbm, MATS, in_sem.at[4]),
    ]
    for cp in small + loads:
        cp.start()

    barrier = pltpu.get_barrier_semaphore()
    for t in range(1, nx_dev):
        pl.semaphore_signal(barrier, inc=1, device_id={"gx": px(t)}, device_id_type=MESH)

    for t in (1, ny_dev - 1):
        pl.semaphore_signal(barrier, inc=1, device_id={"gy": py(t)}, device_id_type=MESH)
    for t in range(1, n_chips):
        pl.semaphore_signal(barrier, inc=1, device_id={"gy": chip_at(t)}, device_id_type=MESH)

    for cp in small:
        cp.wait()

    r8 = rows_of((8, 128))
    j8 = lax.rem(lanes((8, 128)), 8)
    den = jnp.zeros((8, 128), f32)
    thk = jnp.zeros((8, 128), f32)
    for k in range(levels):
        den = jnp.where(r8 == k, den_ref[k], den)
        thk = jnp.where(r8 == k, thk_ref[k], thk)

    def lift(a):
        return jnp.where(r8 == 7, a, roll(a, -1, 0))

    def below(a):
        return jnp.where(r8 == 0, 0.0, roll(a, 1, 0))

    lden = lift(den)
    fd = (den + lden) / 2.0
    fs = (thk + lift(thk)) / 2.0
    mass = den * thk
    zw = (DT / 60.0) / (fd * fs)
    zt = (DT / 60.0) / mass
    sc = (1.0 / DT) / mass
    coefs = [lden * zw, below(lden) * zw, fd * zt, below(fd) * zt, fd * sc, below(fd) * sc, DT / fs]
    for i, a in enumerate(coefs):
        COEF[i * 8 : i * 8 + 8, :] = jnp.concatenate([a, a], axis=1)

    cond = fd / fs
    diag = jnp.sqrt(cond / mass)
    off = -jnp.sqrt(cond / lift(mass))
    b_mat = jnp.where(j8 == r8, diag, jnp.where(j8 == r8 + 1, off, 0.0))
    q_mat = jnp.where(j8 == r8, 1.0, 0.0)
    pairs = [
        (4, j8 < 4),
        (1, lax.rem(j8, 2) == 0), (1, lax.rem(j8, 2) == 1),
        (3, lax.rem(j8, 2) == 0), (3, lax.rem(j8, 2) == 1),
        (2, lax.rem(j8, 4) < 2), (2, lax.rem(j8, 4) >= 2),
    ]

    def total(x):
        return ((x[0] + x[1]) + (x[2] + x[3])) + ((x[4] + x[5]) + (x[6] + x[7]))

    def partner(x, o, ahead):
        if o == 4:
            return roll(x, 4, 1)
        return jnp.where(ahead, roll(x, -o, 1), roll(x, o, 1))

    def sweep(_, carry):
        b, q = list(carry[:8]), list(carry[8:])
        for o, ahead in pairs:
            bp = [partner(x, o, ahead) for x in b]
            al = total([x * x for x in b])
            ap = total([x * x for x in bp])
            g = total([x * y for x, y in zip(b, bp)])
            d = ap - al
            h2 = d * d + 4.0 * g * g
            ok = h2 > 1e-30
            rh = lax.rsqrt(jnp.where(ok, h2, 1.0))
            c2 = 0.5 + 0.5 * jnp.abs(d) * rh
            rc = lax.rsqrt(c2)
            sg = jnp.where(d > 0.0, g, jnp.where(d < 0.0, -g, jnp.where(ahead, g, -g)))
            c = jnp.where(ok, c2 * rc, 1.0)
            s = jnp.where(ok, sg * rh * rc, 0.0)
            qp = [partner(x, o, ahead) for x in q]
            b = [c * x - s * y for x, y in zip(b, bp)]
            q = [c * x - s * y for x, y in zip(q, qp)]
        return (*b, *q)

    start = [jnp.broadcast_to(m[k : k + 1], (8, 128)) for m in (b_mat, q_mat) for k in range(8)]
    got = lax.fori_loop(0, 1, sweep, tuple(start))

    for cp in loads[:4]:
        cp.wait()
    lane_c = lanes((YC, 128))

    @pl.loop(0, chunks)
    def _(c):
        y0 = pl.multiple_of(c * YC, YC)
        east = jnp.zeros((YC, 128), f32)
        west = jnp.zeros((YC, 128), f32)
        for k in range(levels):
            o = 16 * k
            rows = pl.ds(y0 + 8, YC)
            wl, wr = W[k, rows, 0:128], W[k, rows, 128:256]
            tl, tr = TH[k, rows, 0:128], TH[k, rows, 128:256]
            ur = U[k, pl.ds(y0, YC), 128:256]
            east = jnp.where((lane_c >= o) & (lane_c < o + 3), roll(wr, o - 125, 1), east)
            east = jnp.where((lane_c >= o + 3) & (lane_c < o + 6), roll(tr, o + 3 - 125, 1), east)
            east = jnp.where(lane_c == o + 6, roll(ur, o + 6 - 127, 1), east)
            west = jnp.where((lane_c >= o) & (lane_c < o + 3), roll(wl, o, 1), west)
            west = jnp.where((lane_c >= o + 3) & (lane_c < o + 6), roll(tl, o + 3, 1), west)
        PE_S[pl.ds(y0, YC), :] = east
        PW_S[pl.ds(y0, YC), :] = west

    for k in range(levels):
        a, b, c = W[k, ny : ny + 8, :], TH[k, ny : ny + 8, :], V[k, ny : ny + 8, :]
        row = rows_of((8, nx))
        YN_S[k] = jnp.where(row < 3, roll(a, 3, 0), jnp.where(row < 6, roll(b, 6, 0), roll(c, 7, 0)))
        a, b = W[k, 8:16, :], TH[k, 8:16, :]
        YS_S[k] = jnp.where(row < 3, a, roll(b, 3, 0))

    pl.semaphore_wait(barrier, nx_dev - 1 + 2 + n_chips - 1)
    halos = []
    for i, (src, dst, where) in enumerate(
        [
            (PE_S, PE_R, {"gx": px(1)}),
            (PW_S, PW_R, {"gx": px(nx_dev - 1)}),
            (YN_S, YN_R, {"gy": py(1)}),
            (YS_S, YS_R, {"gy": py(ny_dev - 1)}),
        ]
    ):
        cp = pltpu.make_async_remote_copy(
            src_ref=src, dst_ref=dst, send_sem=hs_sem.at[i], recv_sem=hr_sem.at[i],
            device_id=where, device_id_type=MESH,
        )
        cp.start()
        halos.append(cp)

    got = lax.fori_loop(0, 4, sweep, got)
    norm = 1.0 / total([x * x for x in got[8:]])
    lam = total([x * x for x in got[:8]]) * norm
    unit = jnp.sqrt(norm)
    q_mat = jnp.zeros((8, 128), f32)
    for k in range(8):
        q_mat = jnp.where(r8 == k, got[8 + k] * unit, q_mat)
    root = jnp.sqrt(mass)
    qf = q_mat * root
    qi = q_mat / root
    for j in range(8):
        TF[j * 8 : j * 8 + 8, :] = jnp.broadcast_to(qf[:, j : j + 1], (8, 128))
        TI[j * 8 : j * 8 + 8, :] = jnp.broadcast_to(qi[:, j : j + 1], (8, 128))
        LAM[j] = jnp.broadcast_to(lam[:, j : j + 1], (8, 128))

    def nxt(k):
        return min(k + 1, levels - 1)

    def z_part(field, k, rows, w, fz_below, zi):
        zq = [field[min(max(k + s, 0), levels - 1), rows, :] for s in range(-2, 4)]
        fz = flux(*zq, w)
        tend = COEF[zi + k : zi + k + 1, :] * fz
        if k > 0:
            tend = tend - COEF[zi + 8 + k : zi + 9 + k, :] * fz_below
        return tend, fz

    @pl.loop(0, chunks)
    def _(c):
        y0 = pl.multiple_of(c * YC, YC)
        rows = pl.ds(y0 + 8, YC)
        fz = None
        for k in range(levels):
            w, w1 = W[k, rows, :], W[nxt(k), rows, :]
            tend, fz = z_part(W, k, rows, (w + w1) / 2.0, fz, 0)
            WS[k, pl.ds(y0, YC), :] = w - tend + (0.5 * DT) * (TH[k, rows, :] + TH[nxt(k), rows, :])

    for cp in halos:
        cp.wait()

    for k in range(levels):
        n8, s8 = YN_R[k], YS_R[k]
        W[k, 0:8, :] = roll(n8, 5, 0)
        TH[k, 0:8, :] = roll(n8, 2, 0)
        V[k, 0:8, :] = roll(n8, 1, 0)
        W[k, ny + 8 : ny + 16, :] = s8
        TH[k, ny + 8 : ny + 16, :] = roll(s8, 5, 0)

    lane_n = lanes((ny, 128))
    ph, po = PE_R[...], PW_S[...]
    lane_m = lax.rem(lane_n, 16)
    u_th = roll(ph, -3, 1)
    u_top = jnp.where(lane_n >= 112, roll(ph, -6, 1), roll(ph, -22, 1))
    u_w = (roll(ph, -6, 1) + u_top) / 2.0
    FPK[...] = flux(
        ph, roll(ph, -1, 1), roll(ph, -2, 1), po, roll(po, -1, 1), roll(po, -2, 1),
        jnp.where(lane_m == 0, u_w, u_th),
    )

    def y_shifts(block, n):
        return [roll(block, -s, 0)[8 : 8 + n] if s else block[8 : 8 + n] for s in range(-2, 4)]

    def south_flux(field, first, lifted):
        for k in range(levels):
            block = field[k, 0:16, :]
            qs = [roll(block, -s, 0)[0:8] for s in range(-2, 4)]
            c = V[k, 0:8, :]
            if lifted:
                c = (c + V[nxt(k), 0:8, :]) / 2.0
            FYP[k] = flux(*qs, c)

    def horizontal(field, k, y0, extra, lifted):
        o = 16 * k + extra
        rows = pl.ds(y0 + 8, YC)
        cen = pl.ds(y0, YC)
        block = field[k, pl.ds(y0, YC + 16), :]
        q = block[8 : 8 + YC]
        left, right = q[:, :128], q[:, 128:]
        pe, pw = PW_R[cen, :], PE_R[cen, :]
        ls, rs = [], []
        for s in range(-2, 4):
            if s == 0:
                ls.append(left)
                rs.append(right)
                continue
            a, b = roll(left, -s, 1), roll(right, -s, 1)
            if s > 0:
                ls.append(jnp.where(lane_c < 128 - s, a, b))
                rs.append(jnp.where(lane_c < 128 - s, b, roll(pe, -s - o, 1)))
            else:
                ls.append(jnp.where(lane_c >= -s, a, roll(pw, -s - 3 - o, 1)))
                rs.append(jnp.where(lane_c >= -s, b, a))
        u, v = U[k, cen, :], V[k, rows, :]
        if lifted:
            u = (u + U[nxt(k), cen, :]) / 2.0
            v = (v + V[nxt(k), rows, :]) / 2.0
        fl = flux(*ls, u[:, :128])
        fr = flux(*rs, u[:, 128:])
        fl_roll = roll(fl, 1, 1)
        wl = jnp.where(lane_c >= 1, fl_roll, roll(FPK[cen, :], -o, 1))
        wr = jnp.where(lane_c >= 1, roll(fr, 1, 1), fl_roll)
        div = jnp.concatenate([fl - wl, fr - wr], axis=1)
        fy = flux(*y_shifts(block, YC), v)
        prev = roll(jnp.concatenate([FYP[k], fy], axis=0), 1, 0)[8:]
        FYP[k] = fy[YC - 8 :]
        div = div + (fy - prev)
        return (-DT / 60.0) * div

    def send(src, dst, s_sem, r_sem, who):
        return pltpu.make_async_remote_copy(
            src_ref=src, dst_ref=dst, send_sem=s_sem, recv_sem=r_sem,
            device_id=who, device_id_type=MESH,
        )

    south_flux(W, 0, True)

    @pl.loop(0, chunks)
    def _(c):
        y0 = pl.multiple_of(c * YC, YC)
        cen = pl.ds(y0, YC)
        star_below = None
        for k in range(levels):
            star = WS[k, cen, :] + horizontal(W, k, y0, 0, True)
            WS[k, cen, :] = star
            u = U[k, cen, :]
            ul = roll(u[:, :128], 1, 1)
            uw = jnp.where(lane_c >= 1, ul, roll(PE_R[cen, :], -(16 * k + 6), 1))
            ue = jnp.where(lane_c >= 1, roll(u[:, 128:], 1, 1), ul)
            vb = V[k, pl.ds(y0, YC + 8), :]
            dv = (vb - roll(vb, 1, 0))[8:]
            src = (u - jnp.concatenate([uw, ue], axis=1) + dv) * (1.0 / DT)
            src = src + COEF[32 + k : 33 + k, :] * star
            if k > 0:
                src = src - COEF[40 + k : 41 + k, :] * star_below
            star_below = star
            SRC[k] = src
        for h in range(2):
            hs = slice(128 * h, 128 * h + 128)
            col = [SRC[k, :, hs] for k in range(levels)]
            for j in range(levels):
                acc = TF[j * 8 : j * 8 + 1, :] * col[0]
                for k in range(1, levels):
                    acc = acc + TF[j * 8 + k : j * 8 + k + 1, :] * col[k]
                TX1[j, c, h] = acc
        pltpu.make_async_copy(TX1.at[gx, c], RX1.at[c, gx], l1_sem.at[c]).start()
        for t in range(1, nx_dev):
            g = px(t)
            send(TX1.at[g, c], RX1.at[c, gx], s1_sem.at[c, t], r1_sem.at[c, gx], {"gx": g}).start()

    south_flux(TH, 0, False)

    @pl.loop(0, chunks)
    def _(c):
        y0 = pl.multiple_of(c * YC, YC)
        fz = None
        for k in range(levels):
            rows = pl.ds(y0 + 8, YC)
            tend, fz = z_part(TH, k, rows, W[k, rows, :], fz, 16)
            tn_ref[k, pl.ds(y0, YC), :] = TH[k, rows, :] - tend + horizontal(TH, k, y0, 3, False)

    lam_g = LAM[gx]
    rate, scale = [], []
    for h in range(2):
        mu = lam_g + tab_ref[16 + 8 * h : 24 + 8 * h, :]
        rt = jnp.sqrt(mu * mu + 4.0 * mu)
        rate.append(2.0 / (2.0 + mu + rt))
        scale.append(-1.0 / rt)

    loads[4].wait()

    def x_forward(c, carry):
        y0 = pl.multiple_of(c * YC, YC)
        pltpu.make_async_copy(TX1.at[gx, c], RX1.at[c, gx], l1_sem.at[c]).wait()
        for t in range(1, nx_dev):
            g = px(t)
            send(TX1.at[g, c], RX1.at[c, g], s1_sem.at[c, t], r1_sem.at[c, g], {"gx": g}).wait_recv()
        for i in range(YC // 8):
            sub = slice(8 * i, 8 * i + 8)
            x = [RX1[c, q // 2, q % 2, sub, :] for q in range(16)]
            y_0, y_8, re, im = fwd16(x)
            Z[8 * i : 8 * i + 8, 0:128] = y_0
            Z[8 * i : 8 * i + 8, 128:256] = y_8
            for m in range(1, 8):
                co, si = tab_ref[m : m + 1, :], tab_ref[8 + m : 9 + m, :]
                at = m * YC + 8 * i
                Z[at : at + 8, 0:128] = re[m] * co + im[m] * si
                Z[at : at + 8, 128:256] = im[m] * co - re[m] * si
        o0 = dot3(Z[0:YC, :], MATS[2], MATS[3])
        om = dot3(Z[YC : 8 * YC, :], MATS[0], MATS[1])
        for m in range(8):
            val = o0 if m == 0 else om[(m - 1) * YC : m * YC]
            for h in range(2):
                S[h, pl.ds(y0 * 8 + m, YC, stride=8), :] = val[:, 128 * h : 128 * h + 128]
        a0, a1, b0, b1, p0, p1 = carry
        for i in range(YC):
            at = pl.ds(y0 * 8 + 8 * i, 8)
            f0, f1 = S[0, at, :], S[1, at, :]
            a0, a1 = f0 + rate[0] * a0, f1 + rate[1] * a1
            b0, b1 = b0 + p0 * f0, b1 + p1 * f1
            SA[0, at, :], SA[1, at, :] = a0, a1
            PWR[0, at, :], PWR[1, at, :] = p0, p1
            p0, p1 = p0 * rate[0], p1 * rate[1]
        return a0, a1, b0, b1, p0, p1

    zero = jnp.zeros((8, 128), f32)
    one = jnp.ones((8, 128), f32)
    a0, a1, b0, b1, p0, p1 = lax.fori_loop(0, chunks, x_forward, (zero, zero, zero, zero, one, one))

    first = core == 0
    whole = [p0, p1]
    mine = []
    for h, (a, b) in enumerate([(a0, b0), (a1, b1)]):
        IFS[h] = jnp.where(first, a, b)
        mine.append(jnp.where(first, b, a))
    pair = {"gy": gy + 1 - 2 * core}
    swap = send(IFS, IFR, is_sem.at[0], ir_sem.at[0], pair)
    swap.start()
    swap.wait()
    for h in range(2):
        CBS[h] = mine[h] + whole[h] * IFR[h]
    sign = 2 * core - 1
    for t in (4, 12, 11, 5, 3, 13, 10, 6, 2, 14, 8, 9, 7, 1, 15):
        dev = 2 * lax.rem(chip + t * sign + n_chips, n_chips) + core
        send(CBS, CBR.at[t], is_sem.at[1], ir_sem.at[1], {"gy": dev}).start()

    def back(i, carry):
        y = ny - 1 - i
        at = pl.ds(pl.multiple_of(y * 8, 8), 8)
        out = []
        for h in range(2):
            b = rate[h] * carry[h]
            SB[h, at, :] = SA[h, at, :] + b
            out.append(S[h, at, :] + b)
        return tuple(out)

    lax.fori_loop(0, ny, back, (zero, zero), unroll=8)

    others = pl.ds(1, n_chips - 1)
    send(CBR.at[others], CBR.at[others], is_sem.at[1], ir_sem.at[1], pair).wait()
    into = []
    for h in range(2):
        ratio = whole[h] * whole[h]
        acc = CBS[h]
        for t in range(n_chips - 1, 0, -1):
            acc = CBR[t, h] + ratio * acc
        full = ratio
        n = 1
        while n < n_chips:
            full = full * full
            n *= 2
        into.append(acc / (1.0 - full))
        INS[h] = into[h]
    swap = send(INS, INR, is_sem.at[2], ir_sem.at[2], pair)
    swap.start()
    swap.wait()
    ain, bin_ = [], []
    for h in range(2):
        own = IFR[h] + whole[h] * into[h]
        ain.append(jnp.where(first, INR[h], own))
        bin_.append(jnp.where(first, own, INR[h]))
    ra = [rate[h] * ain[h] for h in range(2)]
    rb = [rate[h] * bin_[h] for h in range(2)]

    def correct(y0, n):
        for i in range(n):
            at = pl.ds(y0 * 8 + 8 * i, 8)
            mirror = pl.ds((ny - 1 - i) * 8 - y0 * 8, 8)
            for h in range(2):
                S[h, at, :] = scale[h] * (SB[h, at, :] + PWR[h, at, :] * ra[h] + PWR[h, mirror, :] * rb[h])

    end = slice((ny - 1) * 8, ny * 8)
    for h in range(2):
        last = SA[h, end, :] + PWR[h, end, :] * ra[h]
        S[h, ny * 8 : ny * 8 + 8, :] = scale[h] * (rate[h] * last + bin_[h])
        S[h, ny * 8 + 8 : ny * 8 + 64, :] = jnp.zeros((56, 128), f32)

    def x_inverse(y0, n, put):
        for m in range(8):
            for h in range(2):
                Z[m * n : m * n + n, 128 * h : 128 * h + 128] = S[h, pl.ds(y0 * 8 + m, n, stride=8), :]
        o0 = dot3(Z[0:n, :], MATS[6], MATS[7])
        om = dot3(Z[n : 8 * n, :], MATS[4], MATS[5])
        Z[0:n, :] = o0
        Z[n : 8 * n, :] = om
        for i in range(n // 8):
            zr, zi = {}, {}
            for m in range(1, 8):
                co, si = tab_ref[m : m + 1, :], tab_ref[8 + m : 9 + m, :]
                at = m * n + 8 * i
                a, b = Z[at : at + 8, 0:128], Z[at : at + 8, 128:256]
                zr[m] = a * co - b * si
                zi[m] = a * si + b * co
            put(i, inv16(Z[8 * i : 8 * i + 8, 0:128], Z[8 * i : 8 * i + 8, 128:256], zr, zi))

    lane_8 = lanes((8, 128))

    @pl.loop(0, chunks)
    def _(c):
        y0 = pl.multiple_of(c * YC, YC)

        def put(i, x):
            edge = jnp.zeros((8, 128), f32)
            for q in range(16):
                TX2[q // 2, c, q % 2, 8 * i : 8 * i + 8, :] = x[q]
            for d in range(nx_dev):
                edge = jnp.where(lane_8 == d, roll(x[(2 * d + 2) % 16], d, 1), edge)
            EW[pl.ds(y0 + 8 * i, 8), :] = edge

        correct(y0, YC)
        x_inverse(y0, YC, put)
        pltpu.make_async_copy(TX2.at[gx, c], RX2.at[c, gx], l2_sem.at[c]).start()
        for t in range(1, nx_dev):
            g = px(t)
            send(TX2.at[g, c], RX2.at[c, gx], s2_sem.at[c, t], r2_sem.at[c, gx], {"gx": g}).start()

    EW[ny:128, :] = jnp.zeros((128 - ny, 128), f32)
    ewt = jnp.transpose(EW[...])
    row8 = rows_of((8, 128))

    def put_north(i, x):
        for d in range(nx_dev):
            e = jnp.broadcast_to(ewt[d : d + 1, :], (8, 128))
            n0 = jnp.broadcast_to(x[2 * d][0:1], (8, 128))
            n1 = jnp.broadcast_to(x[2 * d + 1][0:1], (8, 128))
            X2[d] = jnp.where(row8 == 0, n0, jnp.where(row8 == 1, n1, e))

    x_inverse(ny, 8, put_north)
    pltpu.make_async_copy(X2.at[gx], XR.at[gx], l2_sem.at[chunks]).start()
    for t in range(1, nx_dev):
        g = px(t)
        send(X2.at[g], XR.at[gx], sx_sem.at[t], rx_sem.at[gx], {"gx": g}).start()

    @pl.loop(0, chunks)
    def _(c):
        pltpu.make_async_copy(TX2.at[gx, c], RX2.at[c, gx], l2_sem.at[c]).wait()
        for t in range(1, nx_dev):
            g = px(t)
            send(TX2.at[g, c], RX2.at[c, g], s2_sem.at[c, t], r2_sem.at[c, g], {"gx": g}).wait_recv()
        cen = pl.ds(pl.multiple_of(c * YC, YC), YC)
        for h in range(2):
            col = [RX2[c, j, h] for j in range(levels)]
            for k in range(levels):
                acc = TI[k : k + 1, :] * col[0]
                for j in range(1, levels):
                    acc = acc + TI[j * 8 + k : j * 8 + k + 1, :] * col[j]
                p_ref[k, cen, 128 * h : 128 * h + 128] = acc
        for k in range(levels):
            g = COEF[48 + k : 49 + k, :]
            step = p_ref[k + 1, cen, :] - p_ref[k, cen, :] if k + 1 < levels else -p_ref[k, cen, :]
            WS[k, cen, :] = WS[k, cen, :] - g * step

    pltpu.make_async_copy(X2.at[gx], XR.at[gx], l2_sem.at[chunks]).wait()
    for t in range(1, nx_dev):
        g = px(t)
        send(X2.at[g], XR.at[g], sx_sem.at[t], rx_sem.at[g], {"gx": g}).wait_recv()

    @pl.loop(0, chunks)
    def _(c):
        for t in range(1, nx_dev):
            g = px(t)
            send(TX1.at[g, c], RX1.at[c, g], s1_sem.at[c, t], r1_sem.at[c, g], {"gx": g}).wait_send()
            send(TX2.at[g, c], RX2.at[c, g], s2_sem.at[c, t], r2_sem.at[c, g], {"gx": g}).wait_send()

    for t in range(1, nx_dev):
        g = px(t)
        send(X2.at[g], XR.at[g], sx_sem.at[t], rx_sem.at[g], {"gx": g}).wait_send()


def finish(
    U, V, WS, tn_ref, p_ref, XR, TI, un_hbm, vn_hbm, wn_hbm, tn_hbm, p_hbm,
    un_ref, vn_ref, EC, EX, tn_sem, out_sem,
):
    levels, ny, nx = U.shape
    theta = pltpu.make_async_copy(tn_ref, tn_hbm, tn_sem.at[0])
    theta.start()
    lane_n = lanes((ny, 128))
    row8 = rows_of((8, 128))

    def out(i, ref, hbm, k):
        return pltpu.make_async_copy(ref.at[k], hbm.at[k], out_sem.at[i, k])

    outs = [(p_ref, p_hbm), (un_ref, un_hbm), (vn_ref, vn_hbm), (WS, wn_hbm)]
    for k in range(levels):
        out(0, p_ref, p_hbm, k).start()
        out(3, WS, wn_hbm, k).start()

    east = jnp.zeros((8, 128), f32)
    for k in range(levels):
        acc = TI[k : k + 1, :] * XR[0]
        for j in range(1, levels):
            acc = acc + TI[j * 8 + k : j * 8 + k + 1, :] * XR[j]
        EX[k] = acc
        east = jnp.where(row8 == k, jnp.broadcast_to(acc[2:3, :], (8, 128)), east)
    EC[0:8, :] = east
    EC[8:128, :] = jnp.zeros((120, 128), f32)
    EC[...] = jnp.transpose(EC[...])

    for k in range(levels):
        p = p_ref[k]
        pleft, pright = p[:, :128], p[:, 128:]
        col = jnp.broadcast_to(EC[0:ny, k : k + 1], (ny, 128))
        a, b = roll(pleft, -1, 1), roll(pright, -1, 1)
        gl = jnp.where(lane_n < 127, a, b) - pleft
        gr = jnp.where(lane_n < 127, b, col) - pright
        un_ref[k] = U[k] - DT * jnp.concatenate([gl, gr], axis=1)
        out(1, un_ref, un_hbm, k).start()
        ex = EX[k]
        north = jnp.concatenate([ex[0:1, :], ex[1:2, :]], axis=1)
        shifted = roll(p, -1, 0)
        shifted = jnp.where(rows_of((ny, nx)) < ny - 1, shifted, jnp.broadcast_to(north, (ny, nx)))
        vn_ref[k] = V[k, 8 : 8 + ny, :] - DT * (shifted - p)
        out(2, vn_ref, vn_hbm, k).start()

    theta.wait()
    for k in range(levels):
        for i, (ref, hbm) in enumerate(outs):
            out(i, ref, hbm, k).wait()


def per_device(u_face, v_face, w_face, theta_field, density, thickness):
    nx_dev = lax.axis_size("gx")
    ny_dev = lax.axis_size("gy")
    levels, ny, nx = u_face.shape
    chunks = ny // YC
    mats, tab = tables()
    vm = pltpu.VMEM
    dma = pltpu.SemaphoreType.DMA
    full = (levels, ny, nx)
    out = jax.ShapeDtypeStruct(full, f32)
    hbm = pl.BlockSpec(memory_space=pltpu.HBM)
    vmem = pl.BlockSpec(memory_space=pltpu.VMEM)
    scratch = [
        pltpu.SMEM((levels,), f32), pltpu.SMEM((levels,), f32), vm((32, 128), f32),
        vm((56, 256), f32),
        vm((levels, ny + 16, nx), f32),
        vm((levels, ny + 16, nx), f32),
        vm((8, 256, 256), bf16),
        vm((64, 128), f32),
        vm((8, 8, 128), f32),
        vm((ny, 128), f32), vm((ny, 128), f32), vm((ny, 128), f32), vm((ny, 128), f32),
        vm((levels, 8, nx), f32), vm((levels, 8, nx), f32),
        vm((levels, 8, nx), f32), vm((levels, 8, nx), f32),
        vm((ny, 128), f32),
        vm((levels, 8, nx), f32),
        vm((levels, YC, nx), f32),
        vm((levels, chunks, 2, YC, 128), f32),
        vm((chunks, nx_dev, 2, YC, 128), f32),
        vm((8 * YC, 256), f32),
        vm((2, (ny + 8) * 8, 128), f32),
        vm((2, ny * 8, 128), f32),
        vm((2, ny * 8, 128), f32),
        vm((2, ny * 8, 128), f32),
        vm((2, 8, 128), f32), vm((2, 8, 128), f32), vm((2, 8, 128), f32),
        vm((ny_dev // 2, 2, 8, 128), f32),
        vm((2, 8, 128), f32), vm((2, 8, 128), f32),
        vm((nx_dev, chunks, 2, YC, 128), f32),
        vm((chunks, levels, 2, YC, 128), f32),
        vm((nx_dev, 8, 128), f32),
        vm((128, 128), f32),
        dma((8,)), dma((4,)), dma((4,)),
        dma((chunks, nx_dev)), dma((chunks, nx_dev)), dma((chunks,)),
        dma((3,)), dma((3,)),
        dma((chunks, nx_dev)), dma((chunks, nx_dev)), dma((chunks + 1,)),
        dma((nx_dev,)), dma((nx_dev,)),
    ]
    mid = pl.pallas_call(
        functools.partial(kernel, nx_dev, ny_dev),
        out_shape=(
            out,
            jax.ShapeDtypeStruct((levels, ny + 8, nx), f32),
            out,
            out,
            out,
            jax.ShapeDtypeStruct((levels, 8, 128), f32),
            jax.ShapeDtypeStruct((64, 128), f32),
        ),
        in_specs=[hbm] * 8,
        out_specs=(vmem,) * 7,
        scratch_shapes=scratch,
        compiler_params=pltpu.CompilerParams(
            collective_id=0, has_side_effects=True, vmem_limit_bytes=36 << 20
        ),
        name="substep",
    )(*(
        pltpu.with_memory_space_constraint(a, pltpu.HBM)
        for a in (density, thickness, jnp.asarray(tab), u_face, v_face, w_face, theta_field, jnp.asarray(mats))
    ))
    return pl.pallas_call(
        finish,
        out_shape=(out,) * 5,
        in_specs=[vmem] * 7,
        out_specs=(hbm,) * 5,
        scratch_shapes=[
            vm(full, f32), vm(full, f32),
            vm((128, 128), f32), vm((levels, 8, 128), f32), dma((1,)), dma((4, levels)),
        ],
        compiler_params=pltpu.CompilerParams(vmem_limit_bytes=24 << 20),
        name="finish",
    )(*mid)


def solution(mesh):
    spec = P(None, "gy", "gx")
    return jax.shard_map(
        per_device,
        mesh=mesh,
        in_specs=(spec, spec, spec, spec, P(), P()),
        out_specs=(spec,) * 5,
        check_vma=False,
    )
```
